256 devices in a mesh: mode: 16 (over z_hi, y), gz: 16 (over z_lo, x, core).
Axes of the slice: x: 4, y: 4, z: 8 (z_hi: 4, z_lo: 2; z = z_hi * 2 + z_lo), core: 2. Of those that a mesh axis runs over, the one named last changes fastest.
Arguments:
- efield: float32 [3, 256, 256, 256], P(None, 'mode', 'gz'), may hold values from -0.6 to 0.6
- hfield: float32 [3, 256, 256, 256], P(None, 'mode', 'gz'), may hold values from -0.6 to 0.6
- polar: float32 [3, 16, 16, 256, 512], P(None, 'gz', 'mode'), may hold values from -1.2 to 1.2
- velocity: float32 [3, 16, 16, 256, 512], P(None, 'gz', 'mode'), may hold values from -0.5 to 0.5
- material: float32 [4, 16, 16, 256], P(None, 'gz', 'mode'), may hold values from 0.05 to 0.5
Outputs:
- new_efield: float32 [3, 256, 256, 256], P(None, 'mode', 'gz')
- new_hfield: float32 [3, 256, 256, 256], P(None, 'mode', 'gz')
- new_polar: float32 [3, 16, 16, 256, 512], P(None, 'gz', 'mode')
- new_velocity: float32 [3, 16, 16, 256, 512], P(None, 'gz', 'mode')
The draws below stay inside these ranges and needn't reach their ends.
All inputs are finite; a program needn't handle non-finite values.
Results may differ from the reference program's by a relative error of at most 0.0001.
Values sent between devices are 32-bit elements; how exact they have to be, the bound alone decides.
A program may use at most 64 MiB of HBM per device.

```python
import math
import jax
import jax.numpy as jnp
from jax import lax

M = 256
R = 256
NA = 512
Z_DEV = 16
STEPS = 2
SUBSTEPS = 4
NZ = 256
N_GZ = 16


def level_of(stream_key, shape, split, low, top_value):
    gain = 1.0
    for position, blocks in split:
        draws = jax.random.uniform(jax.random.fold_in(jax.random.fold_in(stream_key, 6), position), (blocks,), jnp.float32, low / len(split), top_value / len(split))
        gain = gain * jnp.repeat(jnp.exp(draws), shape[position] // blocks).reshape((-1,) + (1,) * (len(shape) - 1 - position))
    return gain


def gaussian(stream_key, dims, spread, reach, split=(), held_as=jnp.bfloat16):
    result = spread * jax.random.normal(stream_key, dims, jnp.float32)
    if split:
        result = result * level_of(stream_key, dims, split, -0.22, 0.18)
    return jnp.clip(result, -reach, reach).astype(held_as)


def setup_inputs(seed: int = 0) -> dict:
    seeds = jax.random.split(jax.random.key(seed), 6)
    efield = gaussian(seeds[0], (3, M, NZ, R), 0.1, 0.6, ((1, 16), (2, 16)), jnp.float32)
    hfield = gaussian(seeds[1], (3, M, NZ, R), 0.1, 0.6, ((1, 16), (2, 16)), jnp.float32)
    polar = gaussian(seeds[2], (3, N_GZ, Z_DEV, R, NA), 0.4, 1.2, ((1, 16), (2, 16)), jnp.float32)
    velocity = gaussian(seeds[3], (3, N_GZ, Z_DEV, R, NA), 0.1, 0.5, ((1, 16), (2, 16)), jnp.float32)
    material = jnp.clip(jnp.exp(math.log(0.5) - 2.3025851 * jax.random.uniform(seeds[4], (4, N_GZ, Z_DEV, R), jnp.float32) ** level_of(seeds[4], (4, N_GZ, Z_DEV, R), ((1, 16), (2, 16)), -0.2, 0.2)), 0.05, 0.5)
    return dict(efield=efield, hfield=hfield, polar=polar, velocity=velocity, material=material)


axial_ratio = 0.5
highest = lax.Precision.HIGHEST


def tables():
    order = jnp.arange(M, dtype=jnp.int32) // 2
    parity = jnp.arange(M, dtype=jnp.int32) % 2
    angles = jnp.arange(NA, dtype=jnp.int32)
    phase = (order[:, None] * angles[None, :]) % NA
    theta = phase.astype(jnp.float32) * (2.0 * math.pi / NA)
    basis = jnp.where(parity[:, None] == 0, jnp.cos(theta), jnp.sin(theta))
    weights = jnp.where(jnp.arange(M, dtype=jnp.int32) == 0, 1.0 / NA, 2.0 / NA).astype(jnp.float32)
    return basis, basis * weights[:, None]


def azimuthal(field, orders):
    count, planes, radii = field.shape
    pairs = field.reshape(count // 2, 2, planes, radii)
    scale = orders.astype(jnp.float32)[:, None, None]
    return jnp.stack([scale * pairs[:, 1], -scale * pairs[:, 0]], axis=1).reshape(field.shape)


def radial_down(field):
    return field - jnp.concatenate([jnp.zeros_like(field[..., :1]), field[..., :-1]], axis=-1)


def radial_up(field):
    return jnp.concatenate([field[..., 1:], jnp.zeros_like(field[..., :1])], axis=-1) - field


def axial_up(field, above):
    return jnp.concatenate([field[:, 1:], above[:, None]], axis=1) - field


def axial_down(field, below):
    return field - jnp.concatenate([below[:, None], field[:, :-1]], axis=1)


def update_magnetic(efield, hfield, above, orders):
    time_step = 0.7 / M
    outer = jnp.arange(R, dtype=jnp.float32) + 1.0
    inner = jnp.arange(R, dtype=jnp.float32) + 0.5
    h_radial = hfield[0] - time_step * azimuthal(efield[2], orders) / outer + axial_ratio * axial_up(efield[1], above[1])
    h_azimuth = hfield[1] - axial_ratio * axial_up(efield[0], above[0]) + time_step * radial_down(efield[2])
    h_axial = hfield[2] - time_step * (radial_down(outer * efield[1]) - azimuthal(efield[0], orders)) / inner
    return jnp.stack([h_radial, h_azimuth, h_axial])


def update_electric(efield, hfield, below, orders, change):
    time_step = 0.7 / M
    outer = jnp.arange(R, dtype=jnp.float32) + 1.0
    inner = jnp.arange(R, dtype=jnp.float32) + 0.5
    e_radial = efield[0] + time_step * azimuthal(hfield[2], orders) / inner - axial_ratio * axial_down(hfield[1], below[1]) - change[0]
    e_azimuth = efield[1] + axial_ratio * axial_down(hfield[0], below[0]) - time_step * radial_up(hfield[2]) - change[1]
    e_axial = efield[2] + time_step * (radial_up(inner * hfield[1]) - azimuthal(hfield[0], orders)) / outer - change[2]
    return jnp.stack([e_radial, e_azimuth, e_axial])


def respond(points, polar, velocity, material):
    stiff = material[0][..., None]
    damping = material[1][..., None]
    couple = material[2][..., None]
    harden = 0.1 * material[3][..., None]
    before = polar
    for substep in range(SUBSTEPS):
        energy = jnp.sum(polar * polar, axis=0, keepdims=True)
        drive = stiff * (couple * points - polar) - harden * energy * polar
        velocity = ((1.0 - 0.5 * damping) * velocity + drive) / (1.0 + 0.5 * damping)
        polar = polar + velocity
    return polar, velocity, polar - before


def reference(efield, hfield, polar, velocity, material):
    basis, project = tables()
    orders = jnp.arange(M // 2, dtype=jnp.int32)
    edge = jnp.zeros((2, M, R), jnp.float32)
    polar_planes = jnp.transpose(polar.reshape(3, NZ, R, NA), (1, 0, 2, 3))
    velocity_planes = jnp.transpose(velocity.reshape(3, NZ, R, NA), (1, 0, 2, 3))
    material_planes = jnp.transpose(material.reshape(4, NZ, R), (1, 0, 2))

    def plane(operands):
        e_plane, p_plane, v_plane, m_plane = operands
        points = jnp.einsum("ckr,kn->crn", e_plane, basis, precision=highest)
        p_next, v_next, change = respond(points, p_plane, v_plane, m_plane)
        modal = jnp.einsum("crn,kn->ckr", change, project, precision=highest)
        return p_next, v_next, modal

    for step in range(STEPS):
        e_planes = jnp.transpose(efield, (2, 0, 1, 3))
        hfield = update_magnetic(efield, hfield, edge, orders)
        polar_planes, velocity_planes, modal = lax.map(plane, (e_planes, polar_planes, velocity_planes, material_planes))
        change = jnp.transpose(modal, (1, 2, 0, 3))
        efield = update_electric(efield, hfield, edge, orders, change)
    new_polar = jnp.transpose(polar_planes, (1, 0, 2, 3)).reshape(3, N_GZ, Z_DEV, R, NA)
    new_velocity = jnp.transpose(velocity_planes, (1, 0, 2, 3)).reshape(3, N_GZ, Z_DEV, R, NA)
    return efield, hfield, new_polar, new_velocity
```

```python
import jax
import jax.numpy as jnp
import ml_dtypes
import numpy as np
from jax import lax
from jax.experimental import pallas as pl
from jax.experimental.pallas import tpu as pltpu
from jax.sharding import PartitionSpec as P

M = 256
R = 256
NA = 512
SUBSTEPS = 4
G = 16
OWN = 16
TIME_STEP = 0.7 / M
RATIO = 0.5
MESH = pl.DeviceIdType.MESH
F32 = jnp.float32
BF16 = jnp.bfloat16


def tables():
    k = np.arange(M)
    phase = (k // 2)[:, None] * np.arange(NA)[None, :] % NA
    theta = 2.0 * np.pi * phase / NA
    basis = np.where((k % 2)[:, None] == 0, np.cos(theta), np.sin(theta))
    high = basis.astype(ml_dtypes.bfloat16)
    low = (basis - high.astype(np.float64)).astype(ml_dtypes.bfloat16)
    return np.stack([high, low])


def split(value):
    high = value.astype(BF16)
    return high, (value - high.astype(F32)).astype(BF16)


def dot3(a, b, dims):
    mul = lambda x, y: lax.dot_general(x, y, (dims, ((), ())), preferred_element_type=F32)
    return mul(a[0], b[0]) + (mul(a[1], b[0]) + mul(a[0], b[1]))


def shift_lanes(value, amount, keep):
    return jnp.where(keep, pltpu.roll(value, amount % value.shape[1], 1), 0.0)


def kernel(
    e_in, h_in, p_in, v_in, mat_in, tab_in,
    e_out, h_out, p_out, v_out,
    e0, h0, h1, x1, e1, h2, x2, c1, c2, f1, f2, ch1, ch2,
    pol, vel, pts, mat, coef, tab, below1, above1, below2, above2,
    load_sem, send_sem, recv_sem, own_sem, halo_send, halo_recv, out_sem,
):
    me = lax.axis_index("mode")
    gz = lax.axis_index("gz")
    zh, y = me // 4, lax.rem(me, 4)
    up, down = lax.rem(gz + 1, G), lax.rem(gz + G - 1, G)

    def each(fn):
        for dz in range(4):
            def body(dy, carry, dz=dz):
                fn(dz * 4 + dy, lax.rem(zh + dz, 4) * 4 + lax.rem(y + dy, 4))
                return carry
            lax.fori_loop(1 if dz == 0 else 0, 4, body, 0)

    loads = [
        pltpu.make_async_copy(s, d, load_sem.at[i])
        for i, (s, d) in enumerate(
            [(e_in, e0), (h_in, h0), (p_in, pol), (v_in, vel), (mat_in, mat), (tab_in, tab)]
        )
    ]
    for copy in loads:
        copy.start()

    barrier = pltpu.get_barrier_semaphore()
    each(lambda i, p: pl.semaphore_signal(barrier, 1, device_id={"mode": p}, device_id_type=MESH))
    pl.semaphore_signal(barrier, 1, device_id={"gz": up}, device_id_type=MESH)
    pl.semaphore_signal(barrier, 1, device_id={"gz": down}, device_id_type=MESH)
    pl.semaphore_wait(barrier, OWN + 1)

    def exchange(stage, source, target):
        def make(i, p):
            return pltpu.make_async_remote_copy(
                source(p), target, send_sem.at[stage, i], recv_sem.at[stage, i],
                device_id={"mode": p}, device_id_type=MESH,
            )
        own = pltpu.make_async_copy(source(me), target, own_sem.at[stage])

        def start():
            each(lambda i, p: make(i, p).start())
            own.start()

        def wait_recv():
            each(lambda i, p: make(i, p).wait_recv())
            own.wait()

        def wait_send():
            each(lambda i, p: make(i, p).wait_send())

        return start, wait_recv, wait_send

    mine = pl.ds(pl.multiple_of(me * OWN, OWN), OWN)
    rows = lambda p: pl.ds(pl.multiple_of(p * OWN, OWN), OWN)
    go1 = exchange(0, lambda p: e_in.at[:, :, p, :], f1.at[:, mine, :])
    go2 = exchange(1, lambda p: x1.at[:, :, p, :], f2.at[:, mine, :])
    back1 = exchange(2, lambda p: ch1.at[:, rows(p), :], c1.at[:, :, me, :])
    back2 = exchange(3, lambda p: ch2.at[:, rows(p), :], c2.at[:, :, me, :])

    def halo(stage, e, h, below, above):
        def make(i, source, target, to):
            return pltpu.make_async_remote_copy(
                source, target, halo_send.at[stage, i], halo_recv.at[stage, i],
                device_id={"gz": to}, device_id_type=MESH,
            )
        return [
            make(0, e.at[:, :, OWN - 1, :], below.at[0:3], up),
            make(1, h.at[0:2, :, OWN - 1, :], below.at[3:5], up),
            make(2, e.at[0:2, :, 0, :], above, down),
        ]

    go1[0]()
    loads[0].wait()
    loads[1].wait()
    halo1 = halo(0, e0, h0, below1, above1)
    halo2 = halo(1, e1, h1, below2, above2)
    for copy in halo1:
        copy.start()

    lane = lax.broadcasted_iota(jnp.int32, (1, R), 1)
    outer = lane.astype(F32) + 1.0
    inner = lane.astype(F32) + 0.5
    per_outer, per_inner = TIME_STEP / outer, TIME_STEP / inner
    keep_down, keep_up = lane > 0, lane < R - 1
    plane = lax.broadcasted_iota(jnp.int32, (OWN, 1), 0)

    down_r = lambda f: f - shift_lanes(f, 1, keep_down)
    up_r = lambda f: shift_lanes(f, -1, keep_up) - f
    up_z = lambda f, row: jnp.where(plane == OWN - 1, row, pltpu.roll(f, OWN - 1, 0)) - f
    down_z = lambda f, row: f - jnp.where(plane == 0, row, pltpu.roll(f, 1, 0))

    def maxwell(e, h, below, above, h_new, e_new):
        def pair(a, carry):
            order = (me * (OWN // 2) + a).astype(F32)
            signed = (order, -order)
            er, ef, ez, hr, hf, hz = (
                [f[c, 2 * a + s] for s in range(2)] for f in (e, h) for c in range(3)
            )
            ber, bef, bez, bhr, bhf = (
                [below[c, pl.ds(2 * a + s, 1), :] for s in range(2)] for c in range(5)
            )
            edge = lambda c, s: jnp.where(gz == G - 1, 0.0, above[c, pl.ds(2 * a + s, 1), :])
            nr, nf, nz, lr, lf = [], [], [], [], []
            for s in range(2):
                t = 1 - s
                nr.append(hr[s] - (signed[s] * ez[t]) * per_outer + RATIO * up_z(ef[s], edge(1, s)))
                nf.append(hf[s] - RATIO * up_z(er[s], edge(0, s)) + TIME_STEP * down_r(ez[s]))
                nz.append(hz[s] - (down_r(outer * ef[s]) - signed[s] * er[t]) * per_inner)
                r = bhr[s] - (signed[s] * bez[t]) * per_outer + RATIO * (ef[s][0:1] - bef[s])
                f = bhf[s] - RATIO * (er[s][0:1] - ber[s]) + TIME_STEP * down_r(bez[s])
                lr.append(jnp.where(gz == 0, 0.0, r))
                lf.append(jnp.where(gz == 0, 0.0, f))
            for s in range(2):
                t = 1 - s
                k = 2 * a + s
                h_new[0, k], h_new[1, k], h_new[2, k] = nr[s], nf[s], nz[s]
                e_new[0, k] = er[s] + (signed[s] * nz[t]) * per_inner - RATIO * down_z(nf[s], lf[s])
                e_new[1, k] = ef[s] + RATIO * down_z(nr[s], lr[s]) - TIME_STEP * up_r(nz[s])
                e_new[2, k] = ez[s] + (up_r(inner * nf[s]) - signed[s] * nr[t]) * per_outer
            return carry
        lax.fori_loop(0, OWN // 2, pair, 0)

    for copy in halo1:
        copy.wait_recv()
    maxwell(e0, h0, below1, above1, h1, x1)
    go2[0]()

    for copy in loads[2:]:
        copy.wait()
    stiff, damp, couple, harden = (mat[i : i + 1, :] for i in range(4))
    over = 1.0 / (1.0 + 0.5 * damp)
    packed = jnp.concatenate(
        [(1.0 - 0.5 * damp) * over, stiff * couple * over, stiff * over, 0.1 * harden * over]
        + [jnp.zeros((124, R), F32)],
        axis=0,
    )
    for half in range(2):
        turned = packed[:, half * 128 : half * 128 + 128].T
        for i in range(4):
            coef[i, pl.ds(half * 128, 128), :] = jnp.broadcast_to(turned[:, i : i + 1], (128, 128))

    weight = jnp.where(
        lax.broadcasted_iota(jnp.int32, (M, 1), 0) == 0, 1.0 / NA, 2.0 / NA
    ).astype(F32)

    def gas(field, sub, change):
        def forward(c, carry):
            value = field[c] if sub is None else field[c] - sub[c]
            pts[c] = dot3(split(value.T), (tab[0], tab[1]), ((1,), (0,)))
            return carry
        lax.fori_loop(0, 3, forward, 0)

        def block(b, carry):
            at = pl.ds(pl.multiple_of(b * 8, 8), 8)
            keep, drive, pull, soft = (coef[i, at, :] for i in range(4))
            for q in range(NA // 128):
                n = pl.ds(q * 128, 128)
                p = [pol[c, at, n] for c in range(3)]
                v = [vel[c, at, n] for c in range(3)]
                u = [drive * pts[c, at, n] for c in range(3)]
                start = list(p)
                for _ in range(SUBSTEPS):
                    energy = p[0] * p[0] + p[1] * p[1] + p[2] * p[2]
                    rate = pull + soft * energy
                    for c in range(3):
                        v[c] = keep * v[c] + u[c] - rate * p[c]
                        p[c] = p[c] + v[c]
                for c in range(3):
                    pol[c, at, n] = p[c]
                    vel[c, at, n] = v[c]
                    pts[c, at, n] = p[c] - start[c]
            return carry
        lax.fori_loop(0, R // 8, block, 0)

        def backward(c, carry):
            change[c] = weight * dot3((tab[0], tab[1]), split(pts[c]), ((1,), (1,)))
            return carry
        lax.fori_loop(0, 3, backward, 0)

    go1[1]()
    gas(f1, None, ch1)
    back1[0]()

    go2[1]()
    gas(f2, ch1, ch2)
    back2[0]()
    outs = [pltpu.make_async_copy(pol, p_out, out_sem.at[0]), pltpu.make_async_copy(vel, v_out, out_sem.at[1])]
    for copy in outs:
        copy.start()

    back1[1]()

    def subtract(a, b, out):
        def one(i, carry):
            for c in range(3):
                out[c, i] = a[c, i] - b[c, i]
            return carry
        lax.fori_loop(0, OWN, one, 0)

    subtract(x1, c1, e1)
    for copy in halo2:
        copy.start()
    for copy in halo2:
        copy.wait_recv()
    maxwell(e1, h1, below2, above2, h2, x2)
    outs.append(pltpu.make_async_copy(h2, h_out, out_sem.at[2]))
    outs[2].start()

    back2[1]()
    subtract(x2, c2, x2)
    outs.append(pltpu.make_async_copy(x2, e_out, out_sem.at[3]))
    outs[3].start()
    for stage in (go1, go2, back1, back2):
        stage[2]()
    for copy in halo1 + halo2:
        copy.wait_send()
    for copy in outs:
        copy.wait()


def on_device(efield, hfield, polar, velocity, material):
    field = pltpu.VMEM((3, OWN, OWN, R), F32)
    state = pltpu.VMEM((3, R, NA), F32)
    modes = pltpu.VMEM((3, M, R), F32)
    dma = pltpu.SemaphoreType.DMA
    anywhere = pl.BlockSpec(memory_space=pl.ANY)
    new_e, new_h, new_p, new_v = pl.pallas_call(
        kernel,
        out_shape=[
            jax.ShapeDtypeStruct((3, OWN, OWN, R), F32),
            jax.ShapeDtypeStruct((3, OWN, OWN, R), F32),
            jax.ShapeDtypeStruct((3, R, NA), F32),
            jax.ShapeDtypeStruct((3, R, NA), F32),
        ],
        in_specs=[anywhere] * 6,
        out_specs=[anywhere] * 4,
        scratch_shapes=[field] * 9 + [modes] * 4
        + [state] * 3
        + [
            pltpu.VMEM((4, R), F32),
            pltpu.VMEM((4, R, 128), F32),
            pltpu.VMEM((2, M, NA), BF16),
            pltpu.VMEM((5, OWN, R), F32),
            pltpu.VMEM((2, OWN, R), F32),
            pltpu.VMEM((5, OWN, R), F32),
            pltpu.VMEM((2, OWN, R), F32),
            dma((6,)), dma((4, OWN)), dma((4, OWN)), dma((4,)), dma((2, 3)), dma((2, 3)), dma((4,)),
        ],
        compiler_params=pltpu.CompilerParams(
            collective_id=0, has_side_effects=True, vmem_limit_bytes=40 << 20
        ),
        name="yee_gas",
    )(
        efield,
        hfield,
        polar.reshape(3, R, NA),
        velocity.reshape(3, R, NA),
        material.reshape(4, R),
        jnp.asarray(tables()),
    )
    shape = (3, 1, 1, R, NA)
    return new_e, new_h, new_p.reshape(shape), new_v.reshape(shape)


def solution(mesh):
    field, state = P(None, "mode", "gz", None), P(None, "gz", "mode", None, None)
    return jax.shard_map(
        on_device,
        mesh=mesh,
        in_specs=(field, field, state, state, P(None, "gz", "mode", None)),
        out_specs=(field, field, state, state),
        check_vma=False,
    )
```

```python
import jax
import jax.numpy as jnp
import ml_dtypes
import numpy as np
from jax import lax
from jax.experimental import pallas as pl
from jax.experimental.pallas import tpu as pltpu
from jax.sharding import PartitionSpec as P

M = 256
R = 256
NA = 512
SUBSTEPS = 4
G = 16
OWN = 16
TIME_STEP = 0.7 / M
RATIO = 0.5
MESH = pl.DeviceIdType.MESH
F32 = jnp.float32
BF16 = jnp.bfloat16


def tables():
    k = np.arange(M)
    phase = (k // 2)[:, None] * np.arange(NA)[None, :] % NA
    theta = 2.0 * np.pi * phase / NA
    basis = np.where((k % 2)[:, None] == 0, np.cos(theta), np.sin(theta))
    high = basis.astype(ml_dtypes.bfloat16)
    low = (basis - high.astype(np.float64)).astype(ml_dtypes.bfloat16)
    return np.stack([high, low])


def split(value):
    high = value.astype(BF16)
    return high, (value - high.astype(F32)).astype(BF16)


def dot3(a, b, dims):
    mul = lambda x, y: lax.dot_general(x, y, (dims, ((), ())), preferred_element_type=F32)
    return mul(a[0], b[0]) + (mul(a[1], b[0]) + mul(a[0], b[1]))


def shift_lanes(value, amount, keep):
    return jnp.where(keep, pltpu.roll(value, amount % value.shape[1], 1), 0.0)


def kernel(
    e_in, h_in, p_in, v_in, mat_in, tab_in,
    x2, h2, pol, vel,
    e0, h0, h1, x1, e1, c1, c2, f1, f2, ch1, ch2,
    pts, mat, coef, tab, below1, above1, below2, above2,
    load_sem, send_sem, recv_sem, own_sem, halo_send, halo_recv,
):
    me = lax.axis_index("mode")
    gz = lax.axis_index("gz")
    zh, y = me // 4, lax.rem(me, 4)
    up, down = lax.rem(gz + 1, G), lax.rem(gz + G - 1, G)

    def each(fn):
        for dz in range(4):
            def body(dy, carry, dz=dz):
                fn(dz * 4 + dy, lax.rem(zh + dz, 4) * 4 + lax.rem(y + dy, 4))
                return carry
            lax.fori_loop(1 if dz == 0 else 0, 4, body, 0)

    loads = [
        pltpu.make_async_copy(s, d, load_sem.at[i])
        for i, (s, d) in enumerate(
            [(e_in, e0), (h_in, h0), (p_in, pol), (v_in, vel), (mat_in, mat), (tab_in, tab)]
        )
    ]
    for copy in loads:
        copy.start()

    barrier = pltpu.get_barrier_semaphore()
    each(lambda i, p: pl.semaphore_signal(barrier, 1, device_id={"mode": p}, device_id_type=MESH))
    pl.semaphore_signal(barrier, 1, device_id={"gz": up}, device_id_type=MESH)
    pl.semaphore_signal(barrier, 1, device_id={"gz": down}, device_id_type=MESH)
    pl.semaphore_wait(barrier, OWN + 1)

    def exchange(stage, source, target):
        def make(i, p):
            return pltpu.make_async_remote_copy(
                source(p), target, send_sem.at[stage, i], recv_sem.at[stage, i],
                device_id={"mode": p}, device_id_type=MESH,
            )
        own = pltpu.make_async_copy(source(me), target, own_sem.at[stage])

        def start():
            each(lambda i, p: make(i, p).start())
            own.start()

        def wait_recv():
            each(lambda i, p: make(i, p).wait_recv())
            own.wait()

        def wait_send():
            each(lambda i, p: make(i, p).wait_send())

        return start, wait_recv, wait_send

    mine = pl.ds(pl.multiple_of(me * OWN, OWN), OWN)
    rows = lambda p: pl.ds(pl.multiple_of(p * OWN, OWN), OWN)
    go1 = exchange(0, lambda p: e_in.at[:, :, p, :], f1.at[:, mine, :])
    go2 = exchange(1, lambda p: x1.at[:, :, p, :], f2.at[:, mine, :])
    back1 = exchange(2, lambda p: ch1.at[:, rows(p), :], c1.at[:, :, me, :])
    back2 = exchange(3, lambda p: ch2.at[:, rows(p), :], c2.at[:, :, me, :])

    def halo(stage, e, h, below, above):
        def make(i, source, target, to):
            return pltpu.make_async_remote_copy(
                source, target, halo_send.at[stage, i], halo_recv.at[stage, i],
                device_id={"gz": to}, device_id_type=MESH,
            )
        return [
            make(0, e.at[:, :, OWN - 1, :], below.at[0:3], up),
            make(1, h.at[0:2, :, OWN - 1, :], below.at[3:5], up),
            make(2, e.at[0:2, :, 0, :], above, down),
        ]

    go1[0]()
    loads[0].wait()
    loads[1].wait()
    halo1 = halo(0, e0, h0, below1, above1)
    halo2 = halo(1, e1, h1, below2, above2)
    for copy in halo1:
        copy.start()

    lane = lax.broadcasted_iota(jnp.int32, (1, R), 1)
    outer = lane.astype(F32) + 1.0
    inner = lane.astype(F32) + 0.5
    per_outer, per_inner = TIME_STEP / outer, TIME_STEP / inner
    keep_down, keep_up = lane > 0, lane < R - 1
    plane = lax.broadcasted_iota(jnp.int32, (OWN, 1), 0)

    down_r = lambda f: f - shift_lanes(f, 1, keep_down)
    up_r = lambda f: shift_lanes(f, -1, keep_up) - f
    up_z = lambda f, row: jnp.where(plane == OWN - 1, row, pltpu.roll(f, OWN - 1, 0)) - f
    down_z = lambda f, row: f - jnp.where(plane == 0, row, pltpu.roll(f, 1, 0))

    def maxwell(e, h, below, above, h_new, e_new):
        def pair(a, carry):
            order = (me * (OWN // 2) + a).astype(F32)
            signed = (order, -order)
            er, ef, ez, hr, hf, hz = (
                [f[c, 2 * a + s] for s in range(2)] for f in (e, h) for c in range(3)
            )
            ber, bef, bez, bhr, bhf = (
                [below[c, pl.ds(2 * a + s, 1), :] for s in range(2)] for c in range(5)
            )
            edge = lambda c, s: jnp.where(gz == G - 1, 0.0, above[c, pl.ds(2 * a + s, 1), :])
            nr, nf, nz, lr, lf = [], [], [], [], []
            for s in range(2):
                t = 1 - s
                nr.append(hr[s] - (signed[s] * ez[t]) * per_outer + RATIO * up_z(ef[s], edge(1, s)))
                nf.append(hf[s] - RATIO * up_z(er[s], edge(0, s)) + TIME_STEP * down_r(ez[s]))
                nz.append(hz[s] - (down_r(outer * ef[s]) - signed[s] * er[t]) * per_inner)
                r = bhr[s] - (signed[s] * bez[t]) * per_outer + RATIO * (ef[s][0:1] - bef[s])
                f = bhf[s] - RATIO * (er[s][0:1] - ber[s]) + TIME_STEP * down_r(bez[s])
                lr.append(jnp.where(gz == 0, 0.0, r))
                lf.append(jnp.where(gz == 0, 0.0, f))
            for s in range(2):
                t = 1 - s
                k = 2 * a + s
                h_new[0, k], h_new[1, k], h_new[2, k] = nr[s], nf[s], nz[s]
                e_new[0, k] = er[s] + (signed[s] * nz[t]) * per_inner - RATIO * down_z(nf[s], lf[s])
                e_new[1, k] = ef[s] + RATIO * down_z(nr[s], lr[s]) - TIME_STEP * up_r(nz[s])
                e_new[2, k] = ez[s] + (up_r(inner * nf[s]) - signed[s] * nr[t]) * per_outer
            return carry
        lax.fori_loop(0, OWN // 2, pair, 0)

    for copy in halo1:
        copy.wait_recv()
    maxwell(e0, h0, below1, above1, h1, x1)
    go2[0]()

    for copy in loads[2:]:
        copy.wait()
    stiff, damp, couple, harden = (mat[i, 0] for i in range(4))
    over = 1.0 / (1.0 + 0.5 * damp)
    packed = jnp.concatenate(
        [(1.0 - 0.5 * damp) * over, stiff * couple * over, stiff * over, 0.1 * harden * over]
        + [jnp.zeros((124, R), F32)],
        axis=0,
    )
    for half in range(2):
        turned = packed[:, half * 128 : half * 128 + 128].T
        for i in range(4):
            coef[i, pl.ds(half * 128, 128), :] = jnp.broadcast_to(turned[:, i : i + 1], (128, 128))

    weight = jnp.where(
        lax.broadcasted_iota(jnp.int32, (M, 1), 0) == 0, 1.0 / NA, 2.0 / NA
    ).astype(F32)

    def gas(field, sub, change):
        def forward(c, carry):
            value = field[c] if sub is None else field[c] - sub[c]
            pts[c] = dot3(split(value.T), (tab[0], tab[1]), ((1,), (0,)))
            return carry
        lax.fori_loop(0, 3, forward, 0)

        def block(b, carry):
            at = pl.ds(pl.multiple_of(b * 8, 8), 8)
            keep, drive, pull, soft = (coef[i, at, :] for i in range(4))
            for q in range(NA // 128):
                n = pl.ds(q * 128, 128)
                p = [pol[c, at, n] for c in range(3)]
                v = [vel[c, at, n] for c in range(3)]
                u = [drive * pts[c, at, n] for c in range(3)]
                start = list(p)
                for _ in range(SUBSTEPS):
                    energy = p[0] * p[0] + p[1] * p[1] + p[2] * p[2]
                    rate = pull + soft * energy
                    for c in range(3):
                        v[c] = keep * v[c] + u[c] - rate * p[c]
                        p[c] = p[c] + v[c]
                for c in range(3):
                    pol[c, at, n] = p[c]
                    vel[c, at, n] = v[c]
                    pts[c, at, n] = p[c] - start[c]
            return carry
        lax.fori_loop(0, R // 8, block, 0)

        def backward(c, carry):
            change[c] = weight * dot3((tab[0], tab[1]), split(pts[c]), ((1,), (1,)))
            return carry
        lax.fori_loop(0, 3, backward, 0)

    go1[1]()
    gas(f1, None, ch1)
    back1[0]()

    go2[1]()
    gas(f2, ch1, ch2)
    back2[0]()

    back1[1]()

    def subtract(a, b, out):
        def one(i, carry):
            for c in range(3):
                out[c, i] = a[c, i] - b[c, i]
            return carry
        lax.fori_loop(0, OWN, one, 0)

    subtract(x1, c1, e1)
    for copy in halo2:
        copy.start()
    for copy in halo2:
        copy.wait_recv()
    maxwell(e1, h1, below2, above2, h2, x2)

    back2[1]()
    subtract(x2, c2, x2)
    for stage in (go1, go2, back1, back2):
        stage[2]()
    for copy in halo1 + halo2:
        copy.wait_send()


def finish(*refs):
    half, sem = len(refs) // 2, refs[-1]
    copies = [
        pltpu.make_async_copy(refs[i], refs[half + i], sem.at[i]) for i in range(half)
    ]
    for copy in copies:
        copy.start()
    for copy in copies:
        copy.wait()


def on_device(efield, hfield, polar, velocity, material):
    field = pltpu.VMEM((3, OWN, OWN, R), F32)
    state = pltpu.VMEM((3, R, NA), F32)
    modes = pltpu.VMEM((3, M, R), F32)
    dma = pltpu.SemaphoreType.DMA
    anywhere = pl.BlockSpec(memory_space=pl.ANY)
    results = [
        jax.ShapeDtypeStruct((3, OWN, OWN, R), F32),
        jax.ShapeDtypeStruct((3, OWN, OWN, R), F32),
        jax.ShapeDtypeStruct((3, R, NA), F32),
        jax.ShapeDtypeStruct((3, R, NA), F32),
    ]
    made = pl.pallas_call(
        kernel,
        out_shape=[pltpu.VMEM(r.shape, r.dtype) for r in results],
        in_specs=[anywhere] * 6,
        out_specs=[pl.BlockSpec(memory_space=pltpu.VMEM)] * 4,
        scratch_shapes=[field] * 7 + [modes] * 4
        + [state]
        + [
            pltpu.VMEM((4, 1, 1, R), F32),
            pltpu.VMEM((4, R, 128), F32),
            pltpu.VMEM((2, M, NA), BF16),
            pltpu.VMEM((5, OWN, R), F32),
            pltpu.VMEM((2, OWN, R), F32),
            pltpu.VMEM((5, OWN, R), F32),
            pltpu.VMEM((2, OWN, R), F32),
            dma((6,)), dma((4, OWN)), dma((4, OWN)), dma((4,)), dma((2, 3)), dma((2, 3)),
        ],
        compiler_params=pltpu.CompilerParams(
            collective_id=0, has_side_effects=True, vmem_limit_bytes=59 << 20
        ),
        name="yee_gas",
    )(
        efield,
        hfield,
        polar.reshape(3, R, NA),
        velocity.reshape(3, R, NA),
        material,
        jnp.asarray(tables()),
    )
    new_e, new_h, new_p, new_v = pl.pallas_call(
        finish,
        out_shape=results,
        in_specs=[pl.BlockSpec(memory_space=pltpu.VMEM)] * 4,
        out_specs=[anywhere] * 4,
        scratch_shapes=[dma((4,))],
        compiler_params=pltpu.CompilerParams(vmem_limit_bytes=8 << 20),
        name="finish",
    )(*made)
    shape = (3, 1, 1, R, NA)
    return new_e, new_h, new_p.reshape(shape), new_v.reshape(shape)


def solution(mesh):
    field, state = P(None, "mode", "gz", None), P(None, "gz", "mode", None, None)
    return jax.shard_map(
        on_device,
        mesh=mesh,
        in_specs=(field, field, state, state, P(None, "gz", "mode", None)),
        out_specs=(field, field, state, state),
        check_vma=False,
    )
```

```python
import jax
import jax.numpy as jnp
import ml_dtypes
import numpy as np
from jax import lax
from jax.experimental import pallas as pl
from jax.experimental.pallas import tpu as pltpu
from jax.sharding import PartitionSpec as P

M = 256
R = 256
NA = 512
SUBSTEPS = 4
G = 16
OWN = 16
TIME_STEP = 0.7 / M
RATIO = 0.5
MESH = pl.DeviceIdType.MESH
F32 = jnp.float32
BF16 = jnp.bfloat16


def tables():
    k = np.arange(M)
    phase = (k // 2)[:, None] * np.arange(NA)[None, :] % NA
    theta = 2.0 * np.pi * phase / NA
    basis = np.where((k % 2)[:, None] == 0, np.cos(theta), np.sin(theta))
    high = basis.astype(ml_dtypes.bfloat16)
    low = (basis - high.astype(np.float64)).astype(ml_dtypes.bfloat16)
    return np.stack([high, low])


def split(value):
    high = value.astype(BF16)
    return high, (value - high.astype(F32)).astype(BF16)


def dot3(a, b, dims):
    mul = lambda x, y: lax.dot_general(x, y, (dims, ((), ())), preferred_element_type=F32)
    return mul(a[0], b[0]) + (mul(a[1], b[0]) + mul(a[0], b[1]))


def shift_lanes(value, amount, keep):
    return jnp.where(keep, pltpu.roll(value, amount % value.shape[1], 1), 0.0)


def kernel(
    e_in, h_in, p_in, v_in, mat_in, tab_in,
    x2, h2, pol, vel,
    e0, h0, h1, x1, e1, c1, c2, curl1, f1, f2, ch1, ch2,
    pts, mat, coef, tab, below1, above1, below2, above2, before,
    load_sem, send_sem, recv_sem, own_sem, halo_send, halo_recv, next_sem,
):
    me = lax.axis_index("mode")
    gz = lax.axis_index("gz")
    zh, y = me // 4, lax.rem(me, 4)
    up, down = lax.rem(gz + 1, G), lax.rem(gz + G - 1, G)

    def each(fn):
        def body(dy, carry):
            for dz in (2, 1, 3, 0):
                def one(dz=dz):
                    fn(dz * 4 + dy, lax.rem(zh + dz, 4) * 4 + lax.rem(y + dy, 4))
                if dz == 0:
                    pl.when(dy > 0)(one)
                else:
                    one()
            return carry
        lax.fori_loop(0, 4, body, 0)

    loads = [
        pltpu.make_async_copy(s, d, load_sem.at[i])
        for i, (s, d) in enumerate(
            [(e_in, e0), (h_in, h0), (p_in, pol), (v_in, vel), (mat_in, mat), (tab_in, tab)]
        )
    ]
    for copy in loads:
        copy.start()

    barrier = pltpu.get_barrier_semaphore()
    each(lambda i, p: pl.semaphore_signal(barrier, 1, device_id={"mode": p}, device_id_type=MESH))
    pl.semaphore_signal(barrier, 1, device_id={"gz": up}, device_id_type=MESH)
    pl.semaphore_signal(barrier, 1, device_id={"gz": down}, device_id_type=MESH)
    pl.semaphore_wait(barrier, OWN + 1)

    def exchange(stage, source, target):
        def make(i, p):
            return pltpu.make_async_remote_copy(
                source(p), target, send_sem.at[stage, i], recv_sem.at[stage, i],
                device_id={"mode": p}, device_id_type=MESH,
            )
        own = pltpu.make_async_copy(source(me), target, own_sem.at[stage])

        def start():
            each(lambda i, p: make(i, p).start())
            own.start()

        def wait_recv():
            each(lambda i, p: make(i, p).wait_recv())
            own.wait()

        def wait_send():
            each(lambda i, p: make(i, p).wait_send())

        return start, wait_recv, wait_send

    mine = pl.ds(pl.multiple_of(me * OWN, OWN), OWN)
    rows = lambda p: pl.ds(pl.multiple_of(p * OWN, OWN), OWN)
    go1 = exchange(0, lambda p: e_in.at[:, :, p, :], f1.at[:, mine, :])
    back1 = exchange(2, lambda p: ch1.at[:, rows(p), :], c1.at[:, :, me, :])
    back2 = exchange(3, lambda p: ch2.at[:, rows(p), :], c2.at[:, :, me, :])

    def part(stage, i, p, comps):
        return pltpu.make_async_remote_copy(
            curl1.at[comps, :, p, :], f2.at[comps, mine, :],
            send_sem.at[stage, i], recv_sem.at[stage, i], device_id={"mode": p}, device_id_type=MESH,
        )

    AXIAL, RADIAL, REST = pl.ds(0, 1), pl.ds(1, 1), pl.ds(1, 2)

    def rest(i, p, whole, act):
        pl.when(whole)(lambda: act(part(4, i, p, REST)))
        pl.when(jnp.logical_not(whole))(lambda: act(part(4, i, p, RADIAL)))

    own2 = pltpu.make_async_copy(curl1.at[:, :, me, :], f2.at[:, mine, :], own_sem.at[1])
    follow = pltpu.make_async_remote_copy(
        f2.at[0], before, next_sem.at[0], next_sem.at[1],
        device_id={"mode": jnp.minimum(me + 1, OWN - 1)}, device_id_type=MESH,
    )

    def go2_start():
        own2.start()
        each(lambda i, p: part(1, i, p, AXIAL).start())
        each(lambda i, p: rest(i, p, lax.rem(p, 4) == 0, lambda c: c.start()))

    def go2_wait_axial():
        own2.wait()
        each(lambda i, p: part(1, i, p, AXIAL).wait_recv())

    def go2_wait_rest():
        each(lambda i, p: rest(i, p, y == 0, lambda c: c.wait_recv()))

    def go2_wait_send():
        each(lambda i, p: part(1, i, p, AXIAL).wait_send())
        each(lambda i, p: rest(i, p, lax.rem(p, 4) == 0, lambda c: c.wait_send()))

    def halo(stage, e, h, below, above):
        def make(i, source, target, to):
            return pltpu.make_async_remote_copy(
                source, target, halo_send.at[stage, i], halo_recv.at[stage, i],
                device_id={"gz": to}, device_id_type=MESH,
            )
        return [
            make(0, e.at[:, :, OWN - 1, :], below.at[0:3], up),
            make(1, h.at[0:2, :, OWN - 1, :], below.at[3:5], up),
            make(2, e.at[0:2, :, 0, :], above, down),
        ]

    go1[0]()
    loads[0].wait()
    loads[1].wait()
    halo1 = halo(0, e0, h0, below1, above1)
    halo2 = halo(1, e1, h1, below2, above2)
    for copy in halo1:
        copy.start()

    lane = lax.broadcasted_iota(jnp.int32, (1, R), 1)
    outer = lane.astype(F32) + 1.0
    inner = lane.astype(F32) + 0.5
    per_outer, per_inner = TIME_STEP / outer, TIME_STEP / inner
    keep_down, keep_up = lane > 0, lane < R - 1
    plane = lax.broadcasted_iota(jnp.int32, (OWN, 1), 0)

    down_r = lambda f: f - shift_lanes(f, 1, keep_down)
    up_r = lambda f: shift_lanes(f, -1, keep_up) - f
    up_z = lambda f, row: jnp.where(plane == OWN - 1, row, pltpu.roll(f, OWN - 1, 0)) - f
    down_z = lambda f, row: f - jnp.where(plane == 0, row, pltpu.roll(f, 1, 0))

    def maxwell(e, h, below, above, h_new, e_new, curl=None):
        def pair(a, carry):
            order = (me * (OWN // 2) + a).astype(F32)
            signed = (order, -order)
            er, ef, ez, hr, hf, hz = (
                [f[c, 2 * a + s] for s in range(2)] for f in (e, h) for c in range(3)
            )
            ber, bef, bez, bhr, bhf = (
                [below[c, pl.ds(2 * a + s, 1), :] for s in range(2)] for c in range(5)
            )
            edge = lambda c, s: jnp.where(gz == G - 1, 0.0, above[c, pl.ds(2 * a + s, 1), :])
            nr, nf, nz, lr, lf = [], [], [], [], []
            for s in range(2):
                t = 1 - s
                nr.append(hr[s] - (signed[s] * ez[t]) * per_outer + RATIO * up_z(ef[s], edge(1, s)))
                nf.append(hf[s] - RATIO * up_z(er[s], edge(0, s)) + TIME_STEP * down_r(ez[s]))
                nz.append(hz[s] - (down_r(outer * ef[s]) - signed[s] * er[t]) * per_inner)
                r = bhr[s] - (signed[s] * bez[t]) * per_outer + RATIO * (ef[s][0:1] - bef[s])
                f = bhf[s] - RATIO * (er[s][0:1] - ber[s]) + TIME_STEP * down_r(bez[s])
                lr.append(jnp.where(gz == 0, 0.0, r))
                lf.append(jnp.where(gz == 0, 0.0, f))
            made = []
            for s in range(2):
                t = 1 - s
                k = 2 * a + s
                h_new[0, k], h_new[1, k], h_new[2, k] = nr[s], nf[s], nz[s]
                gr = (signed[s] * nz[t]) * per_inner - RATIO * down_z(nf[s], lf[s])
                gf = RATIO * down_z(nr[s], lr[s]) - TIME_STEP * up_r(nz[s])
                gz_ = (up_r(inner * nf[s]) - signed[s] * nr[t]) * per_outer
                e_new[0, k], e_new[1, k], e_new[2, k] = er[s] + gr, ef[s] + gf, ez[s] + gz_
                made.append((gz_, gr, gf))
            if curl is not None:
                for s in range(2):
                    for c in range(3):
                        curl[c, 2 * a + s] = made[s][c]

                @pl.when(me * (OWN // 2) + a == 0)
                def _():
                    curl[0, 1] = made[0][2]
            return carry
        lax.fori_loop(0, OWN // 2, pair, 0)

    for copy in halo1:
        copy.wait_recv()
    maxwell(e0, h0, below1, above1, h1, x1, curl1)
    go2_start()

    for copy in loads[2:]:
        copy.wait()
    stiff, damp, couple, harden = (mat[i, 0] for i in range(4))
    over = 1.0 / (1.0 + 0.5 * damp)
    packed = jnp.concatenate(
        [(1.0 - 0.5 * damp) * over, stiff * couple * over, stiff * over, 0.1 * harden * over]
        + [jnp.zeros((124, R), F32)],
        axis=0,
    )
    for half in range(2):
        turned = packed[:, half * 128 : half * 128 + 128].T
        for i in range(4):
            coef[i, pl.ds(half * 128, 128), :] = jnp.broadcast_to(turned[:, i : i + 1], (128, 128))

    weight = jnp.where(
        lax.broadcasted_iota(jnp.int32, (M, 1), 0) == 0, 1.0 / NA, 2.0 / NA
    ).astype(F32)

    def complete():
        def block(b, carry):
            at = pl.ds(pl.multiple_of(b * OWN, OWN), OWN)
            axial, radial = f2[0, at, :], f2[1, at, :]
            total = up_r(inner * radial) + (RATIO / TIME_STEP) * (outer * (axial - before[at, :]))
            mode = lax.broadcasted_iota(jnp.int32, (OWN, 1), 0) + b * OWN
            order = (mode // 2).astype(F32)
            per_order = jnp.where(mode < 2, 0.0, 1.0 / jnp.maximum(order, 1.0))
            turned = jnp.where(
                lax.rem(mode, 2) == 0, pltpu.roll(total, OWN - 1, 0), -pltpu.roll(total, 1, 0)
            )
            f2[2, at, :] = jnp.where(mode == 0, pltpu.roll(axial, OWN - 1, 0), turned * per_order)
            return carry
        lax.fori_loop(0, M // OWN, block, 0)

    def gas(field, add, sub, change):
        def forward(c, carry):
            value = field[c] if sub is None else field[c] + (add[lax.rem(c + 1, 3)] - sub[c])
            pts[c] = dot3(split(value.T), (tab[0], tab[1]), ((1,), (0,)))
            return carry
        lax.fori_loop(0, 3, forward, 0)

        def block(b, carry):
            at = pl.ds(pl.multiple_of(b * 8, 8), 8)
            keep, drive, pull, soft = (coef[i, at, :] for i in range(4))
            for q in range(NA // 128):
                n = pl.ds(q * 128, 128)
                p = [pol[c, at, n] for c in range(3)]
                v = [vel[c, at, n] for c in range(3)]
                u = [drive * pts[c, at, n] for c in range(3)]
                start = list(p)
                for _ in range(SUBSTEPS):
                    energy = p[0] * p[0] + p[1] * p[1] + p[2] * p[2]
                    rate = pull + soft * energy
                    for c in range(3):
                        v[c] = keep * v[c] + u[c] - rate * p[c]
                        p[c] = p[c] + v[c]
                for c in range(3):
                    pol[c, at, n] = p[c]
                    vel[c, at, n] = v[c]
                    pts[c, at, n] = p[c] - start[c]
            return carry
        lax.fori_loop(0, R // 8, block, 0)

        def backward(c, carry):
            change[c] = weight * dot3((tab[0], tab[1]), split(pts[c]), ((1,), (1,)))
            return carry
        lax.fori_loop(0, 3, backward, 0)

    go1[1]()
    gas(f1, None, None, ch1)
    go2_wait_axial()
    pl.when(y < 3)(lambda: follow.start())
    go2_wait_rest()
    back1[0]()

    @pl.when(y > 0)
    def _():
        follow.wait_recv()
        complete()

    gas(f1, f2, ch1, ch2)
    back2[0]()

    back1[1]()

    def subtract(a, b, out):
        def one(i, carry):
            for c in range(3):
                out[c, i] = a[c, i] - b[c, i]
            return carry
        lax.fori_loop(0, OWN, one, 0)

    subtract(x1, c1, e1)
    for copy in halo2:
        copy.start()
    for copy in halo2:
        copy.wait_recv()
    maxwell(e1, h1, below2, above2, h2, x2)

    back2[1]()
    subtract(x2, c2, x2)
    for stage in (go1, back1, back2):
        stage[2]()
    go2_wait_send()
    pl.when(y < 3)(lambda: follow.wait_send())
    for copy in halo1 + halo2:
        copy.wait_send()


def finish(*refs):
    half, sem = len(refs) // 2, refs[-1]
    copies = [
        pltpu.make_async_copy(refs[i], refs[half + i], sem.at[i]) for i in range(half)
    ]
    for copy in copies:
        copy.start()
    for copy in copies:
        copy.wait()


def on_device(efield, hfield, polar, velocity, material):
    field = pltpu.VMEM((3, OWN, OWN, R), F32)
    state = pltpu.VMEM((3, R, NA), F32)
    modes = pltpu.VMEM((3, M, R), F32)
    dma = pltpu.SemaphoreType.DMA
    anywhere = pl.BlockSpec(memory_space=pl.ANY)
    results = [
        jax.ShapeDtypeStruct((3, OWN, OWN, R), F32),
        jax.ShapeDtypeStruct((3, OWN, OWN, R), F32),
        jax.ShapeDtypeStruct((3, R, NA), F32),
        jax.ShapeDtypeStruct((3, R, NA), F32),
    ]
    made = pl.pallas_call(
        kernel,
        out_shape=[pltpu.VMEM(r.shape, r.dtype) for r in results],
        in_specs=[anywhere] * 6,
        out_specs=[pl.BlockSpec(memory_space=pltpu.VMEM)] * 4,
        scratch_shapes=[field] * 8 + [modes] * 4
        + [state]
        + [
            pltpu.VMEM((4, 1, 1, R), F32),
            pltpu.VMEM((4, R, 128), F32),
            pltpu.VMEM((2, M, NA), BF16),
            pltpu.VMEM((5, OWN, R), F32),
            pltpu.VMEM((2, OWN, R), F32),
            pltpu.VMEM((5, OWN, R), F32),
            pltpu.VMEM((2, OWN, R), F32),
            pltpu.VMEM((M, R), F32),
            dma((6,)), dma((5, OWN)), dma((5, OWN)), dma((4,)), dma((2, 3)), dma((2, 3)), dma((2,)),
        ],
        compiler_params=pltpu.CompilerParams(
            collective_id=0, has_side_effects=True, vmem_limit_bytes=59 << 20
        ),
        name="yee_gas",
    )(
        efield,
        hfield,
        polar.reshape(3, R, NA),
        velocity.reshape(3, R, NA),
        material,
        jnp.asarray(tables()),
    )
    new_e, new_h, new_p, new_v = pl.pallas_call(
        finish,
        out_shape=results,
        in_specs=[pl.BlockSpec(memory_space=pltpu.VMEM)] * 4,
        out_specs=[anywhere] * 4,
        scratch_shapes=[dma((4,))],
        compiler_params=pltpu.CompilerParams(vmem_limit_bytes=8 << 20),
        name="finish",
    )(*made)
    shape = (3, 1, 1, R, NA)
    return new_e, new_h, new_p.reshape(shape), new_v.reshape(shape)


def solution(mesh):
    field, state = P(None, "mode", "gz", None), P(None, "gz", "mode", None, None)
    return jax.shard_map(
        on_device,
        mesh=mesh,
        in_specs=(field, field, state, state, P(None, "gz", "mode", None)),
        out_specs=(field, field, state, state),
        check_vma=False,
    )
```

```python
import jax
import jax.numpy as jnp
import ml_dtypes
import numpy as np
from jax import lax
from jax.experimental import pallas as pl
from jax.experimental.pallas import tpu as pltpu
from jax.sharding import PartitionSpec as P

M = 256
R = 256
NA = 512
SUBSTEPS = 4
G = 16
OWN = 16
TIME_STEP = 0.7 / M
RATIO = 0.5
MESH = pl.DeviceIdType.MESH
F32 = jnp.float32
BF16 = jnp.bfloat16


def tables():
    k = np.arange(M)
    phase = (k // 2)[:, None] * np.arange(NA)[None, :] % NA
    theta = 2.0 * np.pi * phase / NA
    basis = np.where((k % 2)[:, None] == 0, np.cos(theta), np.sin(theta))
    high = basis.astype(ml_dtypes.bfloat16)
    low = (basis - high.astype(np.float64)).astype(ml_dtypes.bfloat16)
    return np.stack([high, low])


def split(value):
    high = value.astype(BF16)
    return high, (value - high.astype(F32)).astype(BF16)


def dot3(a, b, dims):
    mul = lambda x, y: lax.dot_general(x, y, (dims, ((), ())), preferred_element_type=F32)
    return mul(a[0], b[0]) + (mul(a[1], b[0]) + mul(a[0], b[1]))


def shift_lanes(value, amount, keep):
    return jnp.where(keep, pltpu.roll(value, amount % value.shape[1], 1), 0.0)


def kernel(
    e_in, h_in, p_in, v_in, mat_in, tab_in,
    x2, h2, pol, vel,
    e0, h0, h1, x1, e1, c1, c2, curl1, f1, f2, ch1, ch2,
    pts, mat, coef, tab, below1, above1, below2, above2, before, after, psi, gauge_r, gauge_z, relay,
    load_sem, send_sem, recv_sem, own_sem, halo_send, halo_recv, next_sem, relay_send, relay_recv,
):
    me = lax.axis_index("mode")
    gz = lax.axis_index("gz")
    zh, y = me // 4, lax.rem(me, 4)
    up, down = lax.rem(gz + 1, G), lax.rem(gz + G - 1, G)

    def each(fn):
        def body(dy, carry):
            for dz in (2, 1, 3, 0):
                def one(dz=dz):
                    fn(dz * 4 + dy, lax.rem(zh + dz, 4) * 4 + lax.rem(y + dy, 4))
                if dz == 0:
                    pl.when(dy > 0)(one)
                else:
                    one()
            return carry
        lax.fori_loop(0, 4, body, 0)

    loads = [
        pltpu.make_async_copy(s, d, load_sem.at[i])
        for i, (s, d) in enumerate(
            [(e_in, e0), (h_in, h0), (p_in, pol), (v_in, vel), (mat_in, mat), (tab_in, tab)]
        )
    ]
    for copy in loads:
        copy.start()

    def clear(i, carry):
        c1[2, i] = jnp.zeros((OWN, R), F32)
        return carry
    lax.fori_loop(0, OWN, clear, 0)

    barrier = pltpu.get_barrier_semaphore()
    each(lambda i, p: pl.semaphore_signal(barrier, 1, device_id={"mode": p}, device_id_type=MESH))
    pl.semaphore_signal(barrier, 1, device_id={"gz": up}, device_id_type=MESH)
    pl.semaphore_signal(barrier, 1, device_id={"gz": down}, device_id_type=MESH)
    pl.semaphore_wait(barrier, OWN + 1)

    def exchange(stage, source, target):
        def make(i, p):
            return pltpu.make_async_remote_copy(
                source(p), target, send_sem.at[stage, i], recv_sem.at[stage, i],
                device_id={"mode": p}, device_id_type=MESH,
            )
        own = pltpu.make_async_copy(source(me), target, own_sem.at[stage])

        def start():
            each(lambda i, p: make(i, p).start())
            own.start()

        def wait_recv():
            each(lambda i, p: make(i, p).wait_recv())
            own.wait()

        def wait_send():
            each(lambda i, p: make(i, p).wait_send())

        return start, wait_recv, wait_send

    mine = pl.ds(pl.multiple_of(me * OWN, OWN), OWN)
    rows = lambda p: pl.ds(pl.multiple_of(p * OWN, OWN), OWN)
    go1 = exchange(0, lambda p: e_in.at[:, :, p, :], f1.at[:, mine, :])
    back_r = exchange(2, lambda p: gauge_r.at[rows(p), :], c1.at[1, :, me, :])
    back_z = exchange(5, lambda p: gauge_z.at[rows(p), :], c1.at[0, :, me, :])
    back2 = exchange(3, lambda p: ch2.at[:, rows(p), :], c2.at[:, :, me, :])

    def part(stage, i, p, comps):
        return pltpu.make_async_remote_copy(
            curl1.at[comps, :, p, :], f2.at[comps, mine, :],
            send_sem.at[stage, i], recv_sem.at[stage, i], device_id={"mode": p}, device_id_type=MESH,
        )

    AXIAL, RADIAL, REST = pl.ds(0, 1), pl.ds(1, 1), pl.ds(1, 2)

    def rest(i, p, whole, act):
        pl.when(whole)(lambda: act(part(4, i, p, REST)))
        pl.when(jnp.logical_not(whole))(lambda: act(part(4, i, p, RADIAL)))

    def spread(line, to):
        return pltpu.make_async_remote_copy(
            ch1.at[1, rows(to * 4 + line), :], relay.at[to],
            relay_send.at[line * 4 + to], relay_recv.at[to],
            device_id={"mode": zh * 4 + line}, device_id_type=MESH,
        )

    def each_spread(act):
        def body(i, carry):
            act(spread(i // 4, lax.rem(i, 4)))
            return carry
        lax.fori_loop(4, 16, body, 0)

    def relayed(act):
        def body(to, carry):
            act(spread(1, to))
            return carry
        lax.fori_loop(0, 4, body, 0)

    def phi(dz, source):
        to = lax.rem(zh + dz, 4)
        source = ch1.at[1, rows(to * 4), :] if source is None else source.at[to]
        target = c1.at[2, :, zh * 4, :]
        if dz == 0:
            return pltpu.make_async_copy(source, target, own_sem.at[6])
        return pltpu.make_async_remote_copy(
            source, target, send_sem.at[6, dz], recv_sem.at[6, dz],
            device_id={"mode": to * 4 + y}, device_id_type=MESH,
        )

    def each_phi(act):
        for dz in (2, 1, 3, 0):
            pl.when(y == 0)(lambda: act(phi(dz, None), dz))
            pl.when(y > 0)(lambda: act(phi(dz, relay), dz))

    lead = pltpu.make_async_remote_copy(
        psi, after, next_sem.at[2], next_sem.at[3],
        device_id={"mode": jnp.maximum(me - 1, 0)}, device_id_type=MESH,
    )

    own2 = pltpu.make_async_copy(curl1.at[:, :, me, :], f2.at[:, mine, :], own_sem.at[1])
    follow = pltpu.make_async_remote_copy(
        f2.at[0], before, next_sem.at[0], next_sem.at[1],
        device_id={"mode": jnp.minimum(me + 1, OWN - 1)}, device_id_type=MESH,
    )

    def go2_start():
        own2.start()
        each(lambda i, p: part(1, i, p, AXIAL).start())
        each(lambda i, p: rest(i, p, lax.rem(p, 4) == 0, lambda c: c.start()))

    def go2_wait_axial():
        own2.wait()
        each(lambda i, p: part(1, i, p, AXIAL).wait_recv())

    def go2_wait_rest():
        each(lambda i, p: rest(i, p, y == 0, lambda c: c.wait_recv()))

    def go2_wait_send():
        each(lambda i, p: part(1, i, p, AXIAL).wait_send())
        each(lambda i, p: rest(i, p, lax.rem(p, 4) == 0, lambda c: c.wait_send()))

    def halo(stage, e, h, below, above):
        def make(i, source, target, to):
            return pltpu.make_async_remote_copy(
                source, target, halo_send.at[stage, i], halo_recv.at[stage, i],
                device_id={"gz": to}, device_id_type=MESH,
            )
        return [
            make(0, e.at[:, :, OWN - 1, :], below.at[0:3], up),
            make(1, h.at[0:2, :, OWN - 1, :], below.at[3:5], up),
            make(2, e.at[0:2, :, 0, :], above, down),
        ]

    go1[0]()
    loads[0].wait()
    loads[1].wait()
    halo1 = halo(0, e0, h0, below1, above1)
    halo2 = halo(1, e1, h1, below2, above2)
    for copy in halo1:
        copy.start()

    lane = lax.broadcasted_iota(jnp.int32, (1, R), 1)
    outer = lane.astype(F32) + 1.0
    inner = lane.astype(F32) + 0.5
    per_outer, per_inner = TIME_STEP / outer, TIME_STEP / inner
    keep_down, keep_up = lane > 0, lane < R - 1
    plane = lax.broadcasted_iota(jnp.int32, (OWN, 1), 0)

    down_r = lambda f: f - shift_lanes(f, 1, keep_down)
    up_r = lambda f: shift_lanes(f, -1, keep_up) - f
    up_z = lambda f, row: jnp.where(plane == OWN - 1, row, pltpu.roll(f, OWN - 1, 0)) - f
    down_z = lambda f, row: f - jnp.where(plane == 0, row, pltpu.roll(f, 1, 0))

    def maxwell(e, h, below, above, h_new, e_new, curl=None, base=None):
        def pair(a, carry):
            order = (me * (OWN // 2) + a).astype(F32)
            signed = (order, -order)
            er, ef, ez, hr, hf, hz = (
                [f[c, 2 * a + s] for s in range(2)] for f in (e, h) for c in range(3)
            )
            ber, bef, bez, bhr, bhf = (
                [below[c, pl.ds(2 * a + s, 1), :] for s in range(2)] for c in range(5)
            )
            edge = lambda c, s: jnp.where(gz == G - 1, 0.0, above[c, pl.ds(2 * a + s, 1), :])
            nr, nf, nz, lr, lf = [], [], [], [], []
            for s in range(2):
                t = 1 - s
                nr.append(hr[s] - (signed[s] * ez[t]) * per_outer + RATIO * up_z(ef[s], edge(1, s)))
                nf.append(hf[s] - RATIO * up_z(er[s], edge(0, s)) + TIME_STEP * down_r(ez[s]))
                nz.append(hz[s] - (down_r(outer * ef[s]) - signed[s] * er[t]) * per_inner)
                r = bhr[s] - (signed[s] * bez[t]) * per_outer + RATIO * (ef[s][0:1] - bef[s])
                f = bhf[s] - RATIO * (er[s][0:1] - ber[s]) + TIME_STEP * down_r(bez[s])
                lr.append(jnp.where(gz == 0, 0.0, r))
                lf.append(jnp.where(gz == 0, 0.0, f))
            made = []
            for s in range(2):
                t = 1 - s
                k = 2 * a + s
                h_new[0, k], h_new[1, k], h_new[2, k] = nr[s], nf[s], nz[s]
                gr = (signed[s] * nz[t]) * per_inner - RATIO * down_z(nf[s], lf[s])
                gf = RATIO * down_z(nr[s], lr[s]) - TIME_STEP * up_r(nz[s])
                gz_ = (up_r(inner * nf[s]) - signed[s] * nr[t]) * per_outer
                if base is None:
                    e_new[0, k], e_new[1, k], e_new[2, k] = er[s] + gr, ef[s] + gf, ez[s] + gz_
                else:
                    for c, g in enumerate((gr, gf, gz_)):
                        e_new[c, k] = base[c, k] + g
                made.append((gz_, gr, gf))
            if curl is not None:
                for s in range(2):
                    for c in range(3):
                        curl[c, 2 * a + s] = made[s][c]

                @pl.when(me * (OWN // 2) + a == 0)
                def _():
                    curl[0, 1] = made[0][2]
            return carry
        lax.fori_loop(0, OWN // 2, pair, 0)

    for copy in halo1:
        copy.wait_recv()
    maxwell(e0, h0, below1, above1, h1, x1, curl1)
    go2_start()

    for copy in loads[2:]:
        copy.wait()
    stiff, damp, couple, harden = (mat[i, 0] for i in range(4))
    over = 1.0 / (1.0 + 0.5 * damp)
    packed = jnp.concatenate(
        [(1.0 - 0.5 * damp) * over, stiff * couple * over, stiff * over, 0.1 * harden * over]
        + [jnp.zeros((124, R), F32)],
        axis=0,
    )
    for half in range(2):
        turned = packed[:, half * 128 : half * 128 + 128].T
        for i in range(4):
            coef[i, pl.ds(half * 128, 128), :] = jnp.broadcast_to(turned[:, i : i + 1], (128, 128))

    weight = jnp.where(
        lax.broadcasted_iota(jnp.int32, (M, 1), 0) == 0, 1.0 / NA, 2.0 / NA
    ).astype(F32)

    def unrotate(value, b):
        mode = lax.broadcasted_iota(jnp.int32, (OWN, 1), 0) + b * OWN
        per_order = jnp.where(mode < 2, 0.0, 1.0 / jnp.maximum((mode // 2).astype(F32), 1.0))
        turned = jnp.where(
            lax.rem(mode, 2) == 0, -pltpu.roll(value, OWN - 1, 0), pltpu.roll(value, 1, 0)
        )
        return mode, turned * per_order

    def block_rows(b):
        return pl.ds(pl.multiple_of(b * OWN, OWN), OWN)

    def gauge_radial():
        def block(b, carry):
            at = block_rows(b)
            value = jnp.where(y > 0, outer * ch1[1, at, :], 0.0)
            psi[at, :] = value
            gauge_r[at, :] = ch1[0, at, :] - unrotate(down_r(value), b)[1]
            return carry
        lax.fori_loop(0, M // OWN, block, 0)

    def gauge_axial():
        def block(b, carry):
            at = block_rows(b)
            step = jnp.where(y < 3, after[at, :], 0.0) - psi[at, :]
            mode, made = unrotate(step, b)
            value = ch1[2, at, :] - (RATIO / TIME_STEP) * made
            gauge_z[at, :] = jnp.where(mode == 1, pltpu.roll(ch1[1, at, :], 1, 0), value)
            return carry
        lax.fori_loop(0, M // OWN, block, 0)

    def complete():
        def block(b, carry):
            at = pl.ds(pl.multiple_of(b * OWN, OWN), OWN)
            axial, radial = f2[0, at, :], f2[1, at, :]
            total = up_r(inner * radial) + (RATIO / TIME_STEP) * (outer * (axial - before[at, :]))
            mode, made = unrotate(-total, b)
            f2[2, at, :] = jnp.where(mode == 0, pltpu.roll(axial, OWN - 1, 0), made)
            return carry
        lax.fori_loop(0, M // OWN, block, 0)

    def gas(field, add, sub, change):
        def forward(c, carry):
            value = field[c] if sub is None else field[c] + (add[lax.rem(c + 1, 3)] - sub[c])
            pts[c] = dot3(split(value.T), (tab[0], tab[1]), ((1,), (0,)))
            return carry
        lax.fori_loop(0, 3, forward, 0)

        def block(b, carry):
            at = pl.ds(pl.multiple_of(b * 8, 8), 8)
            keep, drive, pull, soft = (coef[i, at, :] for i in range(4))
            for q in range(NA // 128):
                n = pl.ds(q * 128, 128)
                p = [pol[c, at, n] for c in range(3)]
                v = [vel[c, at, n] for c in range(3)]
                u = [drive * pts[c, at, n] for c in range(3)]
                start = list(p)
                for _ in range(SUBSTEPS):
                    energy = p[0] * p[0] + p[1] * p[1] + p[2] * p[2]
                    rate = pull + soft * energy
                    for c in range(3):
                        v[c] = keep * v[c] + u[c] - rate * p[c]
                        p[c] = p[c] + v[c]
                for c in range(3):
                    pol[c, at, n] = p[c]
                    vel[c, at, n] = v[c]
                    pts[c, at, n] = p[c] - start[c]
            return carry
        lax.fori_loop(0, R // 8, block, 0)

        def backward(c, carry):
            made = weight * dot3((tab[0], tab[1]), split(pts[c]), ((1,), (1,)))
            change[c] = made if sub is None else sub[c] + made
            return carry
        lax.fori_loop(0, 3, backward, 0)

    go1[1]()
    gas(f1, None, None, ch1)
    gauge_radial()
    pl.when(y > 0)(lambda: lead.start())
    pl.when(y == 0)(lambda: each_spread(lambda c: c.start()))
    go2_wait_axial()
    pl.when(y < 3)(lambda: follow.start())
    go2_wait_rest()
    back_r[0]()
    pl.when(y < 3)(lambda: lead.wait_recv())
    gauge_axial()
    back_z[0]()
    pl.when(y > 0)(lambda: relayed(lambda c: c.wait_recv()))
    each_phi(lambda c, dz: c.start())

    @pl.when(y > 0)
    def _():
        follow.wait_recv()
        complete()

    gas(f1, f2, ch1, ch2)
    back2[0]()

    back_r[1]()
    back_z[1]()
    each_phi(lambda c, dz: c.wait_recv() if dz else c.wait())

    def subtract(i, carry):
        for c in range(3):
            e1[c, i] = x1[c, i] - c1[(c + 1) % 3, i]
        return carry
    lax.fori_loop(0, OWN, subtract, 0)

    @pl.when(me == 0)
    def _():
        e1[1, 0] = x1[1, 0] - c1[0, 1]
        e1[2, 1] = x1[2, 1]

    for copy in halo2:
        copy.start()
    for copy in halo2:
        copy.wait_recv()
    maxwell(e1, h1, below2, above2, h2, x2, base=x1)

    back2[1]()

    def finish_e(i, carry):
        for c in range(3):
            x2[c, i] = x2[c, i] - c2[c, i]
        return carry
    lax.fori_loop(0, OWN, finish_e, 0)
    for stage in (go1, back_r, back_z, back2):
        stage[2]()
    go2_wait_send()
    pl.when(y < 3)(lambda: follow.wait_send())
    pl.when(y > 0)(lambda: lead.wait_send())
    pl.when(y == 0)(lambda: each_spread(lambda c: c.wait_send()))
    each_phi(lambda c, dz: c.wait_send() if dz else None)
    for copy in halo1 + halo2:
        copy.wait_send()


def finish(*refs):
    half, sem = len(refs) // 2, refs[-1]
    copies = [
        pltpu.make_async_copy(refs[i], refs[half + i], sem.at[i]) for i in range(half)
    ]
    for copy in copies:
        copy.start()
    for copy in copies:
        copy.wait()


def on_device(efield, hfield, polar, velocity, material):
    field = pltpu.VMEM((3, OWN, OWN, R), F32)
    state = pltpu.VMEM((3, R, NA), F32)
    modes = pltpu.VMEM((3, M, R), F32)
    dma = pltpu.SemaphoreType.DMA
    anywhere = pl.BlockSpec(memory_space=pl.ANY)
    results = [
        jax.ShapeDtypeStruct((3, OWN, OWN, R), F32),
        jax.ShapeDtypeStruct((3, OWN, OWN, R), F32),
        jax.ShapeDtypeStruct((3, R, NA), F32),
        jax.ShapeDtypeStruct((3, R, NA), F32),
    ]
    made = pl.pallas_call(
        kernel,
        out_shape=[pltpu.VMEM(r.shape, r.dtype) for r in results],
        in_specs=[anywhere] * 6,
        out_specs=[pl.BlockSpec(memory_space=pltpu.VMEM)] * 4,
        scratch_shapes=[field] * 8 + [modes] * 4
        + [state]
        + [
            pltpu.VMEM((4, 1, 1, R), F32),
            pltpu.VMEM((4, R, 128), F32),
            pltpu.VMEM((2, M, NA), BF16),
            pltpu.VMEM((5, OWN, R), F32),
            pltpu.VMEM((2, OWN, R), F32),
            pltpu.VMEM((5, OWN, R), F32),
            pltpu.VMEM((2, OWN, R), F32),
            pltpu.VMEM((M, R), F32),
            pltpu.VMEM((M, R), F32),
            pltpu.VMEM((M, R), F32),
            pltpu.VMEM((M, R), F32),
            pltpu.VMEM((M, R), F32),
            pltpu.VMEM((4, OWN, R), F32),
            dma((6,)), dma((7, OWN)), dma((7, OWN)), dma((7,)), dma((2, 3)), dma((2, 3)), dma((4,)),
            dma((OWN,)), dma((4,)),
        ],
        compiler_params=pltpu.CompilerParams(
            collective_id=0, has_side_effects=True, vmem_limit_bytes=59 << 20
        ),
        name="yee_gas",
    )(
        efield,
        hfield,
        polar.reshape(3, R, NA),
        velocity.reshape(3, R, NA),
        material,
        jnp.asarray(tables()),
    )
    new_e, new_h, new_p, new_v = pl.pallas_call(
        finish,
        out_shape=results,
        in_specs=[pl.BlockSpec(memory_space=pltpu.VMEM)] * 4,
        out_specs=[anywhere] * 4,
        scratch_shapes=[dma((4,))],
        compiler_params=pltpu.CompilerParams(vmem_limit_bytes=8 << 20),
        name="finish",
    )(*made)
    shape = (3, 1, 1, R, NA)
    return new_e, new_h, new_p.reshape(shape), new_v.reshape(shape)


def solution(mesh):
    field, state = P(None, "mode", "gz", None), P(None, "gz", "mode", None, None)
    return jax.shard_map(
        on_device,
        mesh=mesh,
        in_specs=(field, field, state, state, P(None, "gz", "mode", None)),
        out_specs=(field, field, state, state),
        check_vma=False,
    )
```

```python
import jax
import jax.numpy as jnp
import ml_dtypes
import numpy as np
from jax import lax
from jax.experimental import pallas as pl
from jax.experimental.pallas import tpu as pltpu
from jax.sharding import PartitionSpec as P

M = 256
R = 256
NA = 512
SUBSTEPS = 4
G = 16
OWN = 16
TIME_STEP = 0.7 / M
RATIO = 0.5
MESH = pl.DeviceIdType.MESH
F32 = jnp.float32
BF16 = jnp.bfloat16


def tables():
    k = np.arange(M)
    phase = (k // 2)[:, None] * np.arange(NA)[None, :] % NA
    theta = 2.0 * np.pi * phase / NA
    basis = np.where((k % 2)[:, None] == 0, np.cos(theta), np.sin(theta))
    high = basis.astype(ml_dtypes.bfloat16)
    low = (basis - high.astype(np.float64)).astype(ml_dtypes.bfloat16)
    return np.stack([high, low])


def split(value):
    high = value.astype(BF16)
    return high, (value - high.astype(F32)).astype(BF16)


def dot3(a, b, dims):
    mul = lambda x, y: lax.dot_general(x, y, (dims, ((), ())), preferred_element_type=F32)
    return mul(a[0], b[0]) + (mul(a[1], b[0]) + mul(a[0], b[1]))


def shift_lanes(value, amount, keep):
    return jnp.where(keep, pltpu.roll(value, amount % value.shape[1], 1), 0.0)


def kernel(
    e_in, h_in, p_in, v_in, mat_in, tab_in,
    x2, h2, pol, vel,
    e0, h0, h1, x1, e1, c1, c2, curl1, f1, f2, ch1, ch2,
    pts, mat, coef, tab, below1, above1, below2, above2, before, after, psi, gauge_r, gauge_z, relay,
    load_sem, send_sem, recv_sem, own_sem, halo_send, halo_recv, next_sem, relay_send, relay_recv,
):
    me = lax.axis_index("mode")
    gz = lax.axis_index("gz")
    zh, y = me // 4, lax.rem(me, 4)
    up, down = lax.rem(gz + 1, G), lax.rem(gz + G - 1, G)

    def each(fn):
        def body(dy, carry):
            for dz in (2, 1, 3, 0):
                def one(dz=dz):
                    fn(dz * 4 + dy, lax.rem(zh + dz, 4) * 4 + lax.rem(y + dy, 4))
                if dz == 0:
                    pl.when(dy > 0)(one)
                else:
                    one()
            return carry
        lax.fori_loop(0, 4, body, 0)

    loads = [
        pltpu.make_async_copy(s, d, load_sem.at[i])
        for i, (s, d) in enumerate(
            [(e_in, e0), (h_in, h0), (p_in, pol), (v_in, vel), (mat_in, mat), (tab_in, tab)]
        )
    ]
    for copy in loads:
        copy.start()

    def clear(i, carry):
        c1[2, i] = jnp.zeros((OWN, R), F32)
        return carry
    lax.fori_loop(0, OWN, clear, 0)

    barrier = pltpu.get_barrier_semaphore()
    each(lambda i, p: pl.semaphore_signal(barrier, 1, device_id={"mode": p}, device_id_type=MESH))
    pl.semaphore_signal(barrier, 1, device_id={"gz": up}, device_id_type=MESH)
    pl.semaphore_signal(barrier, 1, device_id={"gz": down}, device_id_type=MESH)
    pl.semaphore_wait(barrier, OWN + 1)

    def exchange(stage, source, target):
        def make(i, p):
            return pltpu.make_async_remote_copy(
                source(p), target, send_sem.at[stage, i], recv_sem.at[stage, i],
                device_id={"mode": p}, device_id_type=MESH,
            )
        own = pltpu.make_async_copy(source(me), target, own_sem.at[stage])

        def start():
            each(lambda i, p: make(i, p).start())
            own.start()

        def wait_recv():
            each(lambda i, p: make(i, p).wait_recv())
            own.wait()

        def wait_send():
            each(lambda i, p: make(i, p).wait_send())

        return start, wait_recv, wait_send

    mine = pl.ds(pl.multiple_of(me * OWN, OWN), OWN)
    rows = lambda p: pl.ds(pl.multiple_of(p * OWN, OWN), OWN)
    go1 = exchange(0, lambda p: e_in.at[:, :, p, :], f1.at[:, mine, :])
    back_r = exchange(2, lambda p: gauge_r.at[rows(p), :], c1.at[1, :, me, :])
    back_z = exchange(5, lambda p: gauge_z.at[rows(p), :], c1.at[0, :, me, :])
    back2 = exchange(3, lambda p: ch2.at[:, rows(p), :], c2.at[:, :, me, :])

    def part(stage, i, p, comps):
        return pltpu.make_async_remote_copy(
            curl1.at[comps, :, p, :], f2.at[comps, mine, :],
            send_sem.at[stage, i], recv_sem.at[stage, i], device_id={"mode": p}, device_id_type=MESH,
        )

    AXIAL, RADIAL, REST = pl.ds(0, 1), pl.ds(1, 1), pl.ds(1, 2)

    def rest(i, p, whole, act):
        pl.when(whole)(lambda: act(part(4, i, p, REST)))
        pl.when(jnp.logical_not(whole))(lambda: act(part(4, i, p, RADIAL)))

    def spread(line, to):
        return pltpu.make_async_remote_copy(
            ch1.at[1, rows(to * 4 + line), :], relay.at[to],
            relay_send.at[line * 4 + to], relay_recv.at[to],
            device_id={"mode": zh * 4 + line}, device_id_type=MESH,
        )

    def each_spread(act):
        def body(i, carry):
            act(spread(i // 4, lax.rem(i, 4)))
            return carry
        lax.fori_loop(4, 16, body, 0)

    def relayed(act):
        def body(to, carry):
            act(spread(1, to))
            return carry
        lax.fori_loop(0, 4, body, 0)

    def phi(dz, source):
        to = lax.rem(zh + dz, 4)
        source = ch1.at[1, rows(to * 4), :] if source is None else source.at[to]
        target = c1.at[2, :, zh * 4, :]
        if dz == 0:
            return pltpu.make_async_copy(source, target, own_sem.at[6])
        return pltpu.make_async_remote_copy(
            source, target, send_sem.at[6, dz], recv_sem.at[6, dz],
            device_id={"mode": to * 4 + y}, device_id_type=MESH,
        )

    def each_phi(act):
        for dz in (2, 1, 3, 0):
            pl.when(y == 0)(lambda: act(phi(dz, None), dz))
            pl.when(y > 0)(lambda: act(phi(dz, relay), dz))

    lead = pltpu.make_async_remote_copy(
        psi, after, next_sem.at[2], next_sem.at[3],
        device_id={"mode": jnp.maximum(me - 1, 0)}, device_id_type=MESH,
    )

    own2 = pltpu.make_async_copy(curl1.at[:, :, me, :], f2.at[:, mine, :], own_sem.at[1])
    follow = pltpu.make_async_remote_copy(
        f2.at[0], before, next_sem.at[0], next_sem.at[1],
        device_id={"mode": jnp.minimum(me + 1, OWN - 1)}, device_id_type=MESH,
    )

    def go2_start():
        own2.start()
        each(lambda i, p: part(1, i, p, AXIAL).start())
        each(lambda i, p: rest(i, p, lax.rem(p, 4) == 0, lambda c: c.start()))

    def go2_wait_axial():
        own2.wait()
        each(lambda i, p: part(1, i, p, AXIAL).wait_recv())

    def go2_wait_rest():
        each(lambda i, p: rest(i, p, y == 0, lambda c: c.wait_recv()))

    def go2_wait_send():
        each(lambda i, p: part(1, i, p, AXIAL).wait_send())
        each(lambda i, p: rest(i, p, lax.rem(p, 4) == 0, lambda c: c.wait_send()))

    def halo(stage, e, h, below, above):
        def make(i, source, target, to):
            return pltpu.make_async_remote_copy(
                source, target, halo_send.at[stage, i], halo_recv.at[stage, i],
                device_id={"gz": to}, device_id_type=MESH,
            )
        return [
            make(0, e.at[:, :, OWN - 1, :], below.at[0:3], up),
            make(1, h.at[0:2, :, OWN - 1, :], below.at[3:5], up),
            make(2, e.at[0:2, :, 0, :], above, down),
        ]

    go1[0]()
    loads[0].wait()
    loads[1].wait()
    halo1 = halo(0, e0, h0, below1, above1)
    halo2 = halo(1, e1, h1, below2, above2)
    for copy in halo1:
        copy.start()

    lane = lax.broadcasted_iota(jnp.int32, (1, R), 1)
    outer = lane.astype(F32) + 1.0
    inner = lane.astype(F32) + 0.5
    per_outer, per_inner = TIME_STEP / outer, TIME_STEP / inner
    keep_down, keep_up = lane > 0, lane < R - 1
    plane = lax.broadcasted_iota(jnp.int32, (OWN, 1), 0)

    down_r = lambda f: f - shift_lanes(f, 1, keep_down)
    up_r = lambda f: shift_lanes(f, -1, keep_up) - f
    up_z = lambda f, row: jnp.where(plane == OWN - 1, row, pltpu.roll(f, OWN - 1, 0)) - f
    down_z = lambda f, row: f - jnp.where(plane == 0, row, pltpu.roll(f, 1, 0))

    def maxwell(e, h, below, above, h_new, e_new, curl=None, base=None):
        def pair(a, carry):
            order = (me * (OWN // 2) + a).astype(F32)
            signed = (order, -order)
            er, ef, ez, hr, hf, hz = (
                [f[c, 2 * a + s] for s in range(2)] for f in (e, h) for c in range(3)
            )
            ber, bef, bez, bhr, bhf = (
                [below[c, pl.ds(2 * a + s, 1), :] for s in range(2)] for c in range(5)
            )
            edge = lambda c, s: jnp.where(gz == G - 1, 0.0, above[c, pl.ds(2 * a + s, 1), :])
            nr, nf, nz, lr, lf = [], [], [], [], []
            for s in range(2):
                t = 1 - s
                nr.append(hr[s] - (signed[s] * ez[t]) * per_outer + RATIO * up_z(ef[s], edge(1, s)))
                nf.append(hf[s] - RATIO * up_z(er[s], edge(0, s)) + TIME_STEP * down_r(ez[s]))
                nz.append(hz[s] - (down_r(outer * ef[s]) - signed[s] * er[t]) * per_inner)
                r = bhr[s] - (signed[s] * bez[t]) * per_outer + RATIO * (ef[s][0:1] - bef[s])
                f = bhf[s] - RATIO * (er[s][0:1] - ber[s]) + TIME_STEP * down_r(bez[s])
                lr.append(jnp.where(gz == 0, 0.0, r))
                lf.append(jnp.where(gz == 0, 0.0, f))
            made = []
            for s in range(2):
                t = 1 - s
                k = 2 * a + s
                h_new[0, k], h_new[1, k], h_new[2, k] = nr[s], nf[s], nz[s]
                gr = (signed[s] * nz[t]) * per_inner - RATIO * down_z(nf[s], lf[s])
                gf = RATIO * down_z(nr[s], lr[s]) - TIME_STEP * up_r(nz[s])
                gz_ = (up_r(inner * nf[s]) - signed[s] * nr[t]) * per_outer
                if base is None:
                    e_new[0, k], e_new[1, k], e_new[2, k] = er[s] + gr, ef[s] + gf, ez[s] + gz_
                else:
                    for c, g in enumerate((gr, gf, gz_)):
                        e_new[c, k] = base[c, k] + g
                made.append((gz_, gr, gf))
            if curl is not None:
                for s in range(2):
                    for c in range(3):
                        curl[c, 2 * a + s] = made[s][c]

                @pl.when(me * (OWN // 2) + a == 0)
                def _():
                    curl[0, 1] = made[0][2]
            return carry
        lax.fori_loop(0, OWN // 2, pair, 0)

    for copy in halo1:
        copy.wait_recv()
    maxwell(e0, h0, below1, above1, h1, x1, curl1)
    go2_start()

    for copy in loads[2:]:
        copy.wait()
    stiff, damp, couple, harden = (mat[i, 0] for i in range(4))
    over = 1.0 / (1.0 + 0.5 * damp)
    packed = jnp.concatenate(
        [(1.0 - 0.5 * damp) * over, stiff * couple * over, stiff * over, 0.1 * harden * over]
        + [jnp.zeros((124, R), F32)],
        axis=0,
    )
    for half in range(2):
        turned = packed[:, half * 128 : half * 128 + 128].T
        for i in range(4):
            coef[i, pl.ds(half * 128, 128), :] = jnp.broadcast_to(turned[:, i : i + 1], (128, 128))

    weight = jnp.where(
        lax.broadcasted_iota(jnp.int32, (M, 1), 0) == 0, 1.0 / NA, 2.0 / NA
    ).astype(F32)

    def unrotate(value, b):
        mode = lax.broadcasted_iota(jnp.int32, (OWN, 1), 0) + b * OWN
        per_order = jnp.where(mode < 2, 0.0, 1.0 / jnp.maximum((mode // 2).astype(F32), 1.0))
        turned = jnp.where(
            lax.rem(mode, 2) == 0, -pltpu.roll(value, OWN - 1, 0), pltpu.roll(value, 1, 0)
        )
        return mode, turned * per_order

    def block_rows(b):
        return pl.ds(pl.multiple_of(b * OWN, OWN), OWN)

    def gauge_psi():
        def block(b, carry):
            at = block_rows(b)
            psi[at, :] = jnp.where(y > 0, outer * ch1[1, at, :], 0.0)
            return carry
        lax.fori_loop(0, M // OWN, block, 0, unroll=4)

    def gauge_radial():
        def block(b, carry):
            at = block_rows(b)
            value = psi[at, :]
            gauge_r[at, :] = ch1[0, at, :] - unrotate(down_r(value), b)[1]
            return carry
        lax.fori_loop(0, M // OWN, block, 0, unroll=4)

    def gauge_axial():
        def block(b, carry):
            at = block_rows(b)
            step = jnp.where(y < 3, after[at, :], 0.0) - psi[at, :]
            mode, made = unrotate(step, b)
            value = ch1[2, at, :] - (RATIO / TIME_STEP) * made
            gauge_z[at, :] = jnp.where(mode == 1, pltpu.roll(ch1[1, at, :], 1, 0), value)
            return carry
        lax.fori_loop(0, M // OWN, block, 0, unroll=4)

    def complete():
        def block(b, carry):
            at = pl.ds(pl.multiple_of(b * OWN, OWN), OWN)
            axial, radial = f2[0, at, :], f2[1, at, :]
            total = up_r(inner * radial) + (RATIO / TIME_STEP) * (outer * (axial - before[at, :]))
            mode, made = unrotate(-total, b)
            f2[2, at, :] = jnp.where(mode == 0, pltpu.roll(axial, OWN - 1, 0), made)
            return carry
        lax.fori_loop(0, M // OWN, block, 0, unroll=4)

    def to_points(field, add, sub, first, last):
        def forward(c, carry):
            value = field[c] if sub is None else field[c] + (add[lax.rem(c + 1, 3)] - sub[c])
            pts[c] = dot3(split(value.T), (tab[0], tab[1]), ((1,), (0,)))
            return carry
        lax.fori_loop(first, last, forward, 0)

    def respond():
        def block(b, carry):
            at = pl.ds(pl.multiple_of(b * 8, 8), 8)
            keep, drive, pull, soft = (coef[i, at, :] for i in range(4))
            for q in range(NA // 128):
                n = pl.ds(q * 128, 128)
                p = [pol[c, at, n] for c in range(3)]
                v = [vel[c, at, n] for c in range(3)]
                u = [drive * pts[c, at, n] for c in range(3)]
                start = list(p)
                for _ in range(SUBSTEPS):
                    energy = p[0] * p[0] + p[1] * p[1] + p[2] * p[2]
                    rate = pull + soft * energy
                    for c in range(3):
                        v[c] = keep * v[c] + u[c] - rate * p[c]
                        p[c] = p[c] + v[c]
                for c in range(3):
                    pol[c, at, n] = p[c]
                    vel[c, at, n] = v[c]
                    pts[c, at, n] = p[c] - start[c]
            return carry
        lax.fori_loop(0, R // 8, block, 0, unroll=2)

    def to_modes(sub, change, first, last):
        def backward(c, carry):
            made = weight * dot3((tab[0], tab[1]), split(pts[c]), ((1,), (1,)))
            change[c] = made if sub is None else sub[c] + made
            return carry
        lax.fori_loop(first, last, backward, 0)

    go1[1]()
    to_points(f1, None, None, 0, 3)
    respond()
    to_modes(None, ch1, 1, 2)
    gauge_psi()
    pl.when(y > 0)(lambda: lead.start())
    pl.when(y == 0)(lambda: each_spread(lambda c: c.start()))
    to_modes(None, ch1, 0, 1)
    to_modes(None, ch1, 2, 3)
    gauge_radial()
    go2_wait_axial()
    pl.when(y < 3)(lambda: follow.start())
    go2_wait_rest()
    back_r[0]()
    pl.when(y < 3)(lambda: lead.wait_recv())
    gauge_axial()
    back_z[0]()
    pl.when(y > 0)(lambda: relayed(lambda c: c.wait_recv()))
    each_phi(lambda c, dz: c.start())
    to_points(f1, f2, ch1, 0, 1)
    to_points(f1, f2, ch1, 2, 3)

    @pl.when(y > 0)
    def _():
        follow.wait_recv()
        complete()

    to_points(f1, f2, ch1, 1, 2)
    respond()
    to_modes(ch1, ch2, 0, 3)
    back2[0]()
    back_r[1]()
    back_z[1]()
    each_phi(lambda c, dz: c.wait_recv() if dz else c.wait())

    def subtract(i, carry):
        for c in range(3):
            e1[c, i] = x1[c, i] - c1[(c + 1) % 3, i]
        return carry
    lax.fori_loop(0, OWN, subtract, 0)

    @pl.when(me == 0)
    def _():
        e1[1, 0] = x1[1, 0] - c1[0, 1]
        e1[2, 1] = x1[2, 1]

    for copy in halo2:
        copy.start()
    for copy in halo2:
        copy.wait_recv()
    maxwell(e1, h1, below2, above2, h2, x2, base=x1)

    back2[1]()

    def finish_e(i, carry):
        for c in range(3):
            x2[c, i] = x2[c, i] - c2[c, i]
        return carry
    lax.fori_loop(0, OWN, finish_e, 0)
    for stage in (go1, back_r, back_z, back2):
        stage[2]()
    go2_wait_send()
    pl.when(y < 3)(lambda: follow.wait_send())
    pl.when(y > 0)(lambda: lead.wait_send())
    pl.when(y == 0)(lambda: each_spread(lambda c: c.wait_send()))
    each_phi(lambda c, dz: c.wait_send() if dz else None)
    for copy in halo1 + halo2:
        copy.wait_send()


def finish(*refs):
    half, sem = len(refs) // 2, refs[-1]
    copies = [
        pltpu.make_async_copy(refs[i], refs[half + i], sem.at[i]) for i in range(half)
    ]
    for copy in copies:
        copy.start()
    for copy in copies:
        copy.wait()


def on_device(efield, hfield, polar, velocity, material):
    field = pltpu.VMEM((3, OWN, OWN, R), F32)
    state = pltpu.VMEM((3, R, NA), F32)
    modes = pltpu.VMEM((3, M, R), F32)
    dma = pltpu.SemaphoreType.DMA
    anywhere = pl.BlockSpec(memory_space=pl.ANY)
    results = [
        jax.ShapeDtypeStruct((3, OWN, OWN, R), F32),
        jax.ShapeDtypeStruct((3, OWN, OWN, R), F32),
        jax.ShapeDtypeStruct((3, R, NA), F32),
        jax.ShapeDtypeStruct((3, R, NA), F32),
    ]
    made = pl.pallas_call(
        kernel,
        out_shape=[pltpu.VMEM(r.shape, r.dtype) for r in results],
        in_specs=[anywhere] * 6,
        out_specs=[pl.BlockSpec(memory_space=pltpu.VMEM)] * 4,
        scratch_shapes=[field] * 8 + [modes] * 4
        + [state]
        + [
            pltpu.VMEM((4, 1, 1, R), F32),
            pltpu.VMEM((4, R, 128), F32),
            pltpu.VMEM((2, M, NA), BF16),
            pltpu.VMEM((5, OWN, R), F32),
            pltpu.VMEM((2, OWN, R), F32),
            pltpu.VMEM((5, OWN, R), F32),
            pltpu.VMEM((2, OWN, R), F32),
            pltpu.VMEM((M, R), F32),
            pltpu.VMEM((M, R), F32),
            pltpu.VMEM((M, R), F32),
            pltpu.VMEM((M, R), F32),
            pltpu.VMEM((M, R), F32),
            pltpu.VMEM((4, OWN, R), F32),
            dma((6,)), dma((7, OWN)), dma((7, OWN)), dma((7,)), dma((2, 3)), dma((2, 3)), dma((4,)),
            dma((OWN,)), dma((4,)),
        ],
        compiler_params=pltpu.CompilerParams(
            collective_id=0, has_side_effects=True, vmem_limit_bytes=59 << 20
        ),
        name="yee_gas",
    )(
        efield,
        hfield,
        polar.reshape(3, R, NA),
        velocity.reshape(3, R, NA),
        material,
        jnp.asarray(tables()),
    )
    new_e, new_h, new_p, new_v = pl.pallas_call(
        finish,
        out_shape=results,
        in_specs=[pl.BlockSpec(memory_space=pltpu.VMEM)] * 4,
        out_specs=[anywhere] * 4,
        scratch_shapes=[dma((4,))],
        compiler_params=pltpu.CompilerParams(vmem_limit_bytes=8 << 20),
        name="finish",
    )(*made)
    shape = (3, 1, 1, R, NA)
    return new_e, new_h, new_p.reshape(shape), new_v.reshape(shape)


def solution(mesh):
    field, state = P(None, "mode", "gz", None), P(None, "gz", "mode", None, None)
    return jax.shard_map(
        on_device,
        mesh=mesh,
        in_specs=(field, field, state, state, P(None, "gz", "mode", None)),
        out_specs=(field, field, state, state),
        check_vma=False,
    )
```

```python
import jax
import jax.numpy as jnp
import ml_dtypes
import numpy as np
from jax import lax
from jax.experimental import pallas as pl
from jax.experimental.pallas import tpu as pltpu
from jax.sharding import PartitionSpec as P

M = 256
R = 256
NA = 512
SUBSTEPS = 4
G = 16
OWN = 16
TIME_STEP = 0.7 / M
RATIO = 0.5
MESH = pl.DeviceIdType.MESH
F32 = jnp.float32
BF16 = jnp.bfloat16


def tables():
    k = np.arange(M)
    phase = (k // 2)[:, None] * np.arange(NA)[None, :] % NA
    theta = 2.0 * np.pi * phase / NA
    basis = np.where((k % 2)[:, None] == 0, np.cos(theta), np.sin(theta))
    high = basis.astype(ml_dtypes.bfloat16)
    low = (basis - high.astype(np.float64)).astype(ml_dtypes.bfloat16)
    return np.stack([high, low])


def split(value):
    high = value.astype(BF16)
    return high, (value - high.astype(F32)).astype(BF16)


def dot3(a, b, dims):
    mul = lambda x, y: lax.dot_general(x, y, (dims, ((), ())), preferred_element_type=F32)
    return mul(a[0], b[0]) + (mul(a[1], b[0]) + mul(a[0], b[1]))


def shift_lanes(value, amount, keep):
    return jnp.where(keep, pltpu.roll(value, amount % value.shape[1], 1), 0.0)


def kernel(
    e_in, h_in, p_in, v_in, mat_in, tab_in,
    x2, h2, pol, vel,
    e0, h0, h1, x1, e1, c1, c2, curl1, f1, f2, ch1, ch2,
    pts, mat, coef, tab, below1, above1, below2, above2, before, after, psi, gauge_r, gauge_z, relay,
    load_sem, send_sem, recv_sem, own_sem, halo_send, halo_recv, next_sem, relay_send, relay_recv,
):
    me = lax.axis_index("mode")
    gz = lax.axis_index("gz")
    zh, y = me // 4, lax.rem(me, 4)
    up, down = lax.rem(gz + 1, G), lax.rem(gz + G - 1, G)

    def each(fn):
        def body(turn, carry):
            dy = lax.rem(turn + 1, 4)
            for dz in (2, 1, 3, 0):
                def one(dz=dz):
                    fn(dz * 4 + dy, lax.rem(zh + dz, 4) * 4 + lax.rem(y + dy, 4))
                if dz == 0:
                    pl.when(dy > 0)(one)
                else:
                    one()
            return carry
        lax.fori_loop(0, 4, body, 0)

    loads = [
        pltpu.make_async_copy(s, d, load_sem.at[i])
        for i, (s, d) in enumerate(
            [(e_in, e0), (h_in, h0), (p_in, pol), (v_in, vel), (mat_in, mat), (tab_in, tab)]
        )
    ]
    for copy in loads:
        copy.start()

    def clear(i, carry):
        c1[2, i] = jnp.zeros((OWN, R), F32)
        return carry
    lax.fori_loop(0, OWN, clear, 0)

    barrier = pltpu.get_barrier_semaphore()
    each(lambda i, p: pl.semaphore_signal(barrier, 1, device_id={"mode": p}, device_id_type=MESH))
    pl.semaphore_signal(barrier, 1, device_id={"gz": up}, device_id_type=MESH)
    pl.semaphore_signal(barrier, 1, device_id={"gz": down}, device_id_type=MESH)
    pl.semaphore_wait(barrier, OWN + 1)

    def exchange(stage, source, target):
        def make(i, p):
            return pltpu.make_async_remote_copy(
                source(p), target, send_sem.at[stage, i], recv_sem.at[stage, i],
                device_id={"mode": p}, device_id_type=MESH,
            )
        own = pltpu.make_async_copy(source(me), target, own_sem.at[stage])

        def start():
            each(lambda i, p: make(i, p).start())
            own.start()

        def wait_recv():
            each(lambda i, p: make(i, p).wait_recv())
            own.wait()

        def wait_send():
            each(lambda i, p: make(i, p).wait_send())

        return start, wait_recv, wait_send

    mine = pl.ds(pl.multiple_of(me * OWN, OWN), OWN)
    rows = lambda p: pl.ds(pl.multiple_of(p * OWN, OWN), OWN)
    go1 = exchange(0, lambda p: e_in.at[:, :, p, :], f1.at[:, mine, :])
    back_r = exchange(2, lambda p: gauge_r.at[rows(p), :], c1.at[1, :, me, :])
    back_z = exchange(5, lambda p: gauge_z.at[rows(p), :], c1.at[0, :, me, :])
    back2 = exchange(3, lambda p: ch2.at[:, rows(p), :], c2.at[:, :, me, :])

    def part(stage, i, p, comps):
        return pltpu.make_async_remote_copy(
            curl1.at[comps, :, p, :], f2.at[comps, mine, :],
            send_sem.at[stage, i], recv_sem.at[stage, i], device_id={"mode": p}, device_id_type=MESH,
        )

    AXIAL, RADIAL, REST = pl.ds(0, 1), pl.ds(1, 1), pl.ds(1, 2)

    def rest(i, p, whole, act):
        pl.when(whole)(lambda: act(part(4, i, p, REST)))
        pl.when(jnp.logical_not(whole))(lambda: act(part(4, i, p, RADIAL)))

    def spread(line, to):
        return pltpu.make_async_remote_copy(
            ch1.at[1, rows(to * 4 + line), :], relay.at[to],
            relay_send.at[line * 4 + to], relay_recv.at[to],
            device_id={"mode": zh * 4 + line}, device_id_type=MESH,
        )

    def each_spread(act):
        def body(i, carry):
            act(spread(i // 4, lax.rem(i, 4)))
            return carry
        lax.fori_loop(4, 16, body, 0)

    def relayed(act):
        def body(to, carry):
            act(spread(1, to))
            return carry
        lax.fori_loop(0, 4, body, 0)

    def phi(dz, source):
        to = lax.rem(zh + dz, 4)
        source = ch1.at[1, rows(to * 4), :] if source is None else source.at[to]
        target = c1.at[2, :, zh * 4, :]
        if dz == 0:
            return pltpu.make_async_copy(source, target, own_sem.at[6])
        return pltpu.make_async_remote_copy(
            source, target, send_sem.at[6, dz], recv_sem.at[6, dz],
            device_id={"mode": to * 4 + y}, device_id_type=MESH,
        )

    def each_phi(act):
        for dz in (2, 1, 3, 0):
            pl.when(y == 0)(lambda: act(phi(dz, None), dz))
            pl.when(y > 0)(lambda: act(phi(dz, relay), dz))

    lead = pltpu.make_async_remote_copy(
        psi, after, next_sem.at[2], next_sem.at[3],
        device_id={"mode": jnp.maximum(me - 1, 0)}, device_id_type=MESH,
    )

    own2 = pltpu.make_async_copy(curl1.at[:, :, me, :], f2.at[:, mine, :], own_sem.at[1])
    follow = pltpu.make_async_remote_copy(
        f2.at[0], before, next_sem.at[0], next_sem.at[1],
        device_id={"mode": jnp.minimum(me + 1, OWN - 1)}, device_id_type=MESH,
    )

    def go2_start():
        own2.start()
        each(lambda i, p: part(1, i, p, AXIAL).start())
        each(lambda i, p: rest(i, p, lax.rem(p, 4) == 0, lambda c: c.start()))

    def go2_wait_axial():
        own2.wait()
        each(lambda i, p: part(1, i, p, AXIAL).wait_recv())

    def go2_wait_rest():
        each(lambda i, p: rest(i, p, y == 0, lambda c: c.wait_recv()))

    def go2_wait_send():
        each(lambda i, p: part(1, i, p, AXIAL).wait_send())
        each(lambda i, p: rest(i, p, lax.rem(p, 4) == 0, lambda c: c.wait_send()))

    def halo(stage, e, h, below, above):
        def make(i, source, target, to):
            return pltpu.make_async_remote_copy(
                source, target, halo_send.at[stage, i], halo_recv.at[stage, i],
                device_id={"gz": to}, device_id_type=MESH,
            )
        return [
            make(0, e.at[:, :, OWN - 1, :], below.at[0:3], up),
            make(1, h.at[0:2, :, OWN - 1, :], below.at[3:5], up),
            make(2, e.at[0:2, :, 0, :], above, down),
        ]

    go1[0]()
    loads[0].wait()
    loads[1].wait()
    halo1 = halo(0, e0, h0, below1, above1)
    halo2 = halo(1, e1, h1, below2, above2)
    for copy in halo1:
        copy.start()

    lane = lax.broadcasted_iota(jnp.int32, (1, R), 1)
    outer = lane.astype(F32) + 1.0
    inner = lane.astype(F32) + 0.5
    per_outer, per_inner = TIME_STEP / outer, TIME_STEP / inner
    keep_down, keep_up = lane > 0, lane < R - 1
    plane = lax.broadcasted_iota(jnp.int32, (OWN, 1), 0)

    down_r = lambda f: f - shift_lanes(f, 1, keep_down)
    up_r = lambda f: shift_lanes(f, -1, keep_up) - f
    up_z = lambda f, row: jnp.where(plane == OWN - 1, row, pltpu.roll(f, OWN - 1, 0)) - f
    down_z = lambda f, row: f - jnp.where(plane == 0, row, pltpu.roll(f, 1, 0))

    def maxwell(e, h, below, above, h_new, e_new, curl=None, base=None):
        def pair(a, carry):
            order = (me * (OWN // 2) + a).astype(F32)
            signed = (order, -order)
            er, ef, ez, hr, hf, hz = (
                [f[c, 2 * a + s] for s in range(2)] for f in (e, h) for c in range(3)
            )
            ber, bef, bez, bhr, bhf = (
                [below[c, pl.ds(2 * a + s, 1), :] for s in range(2)] for c in range(5)
            )
            edge = lambda c, s: jnp.where(gz == G - 1, 0.0, above[c, pl.ds(2 * a + s, 1), :])
            nr, nf, nz, lr, lf = [], [], [], [], []
            for s in range(2):
                t = 1 - s
                nr.append(hr[s] - (signed[s] * ez[t]) * per_outer + RATIO * up_z(ef[s], edge(1, s)))
                nf.append(hf[s] - RATIO * up_z(er[s], edge(0, s)) + TIME_STEP * down_r(ez[s]))
                nz.append(hz[s] - (down_r(outer * ef[s]) - signed[s] * er[t]) * per_inner)
                r = bhr[s] - (signed[s] * bez[t]) * per_outer + RATIO * (ef[s][0:1] - bef[s])
                f = bhf[s] - RATIO * (er[s][0:1] - ber[s]) + TIME_STEP * down_r(bez[s])
                lr.append(jnp.where(gz == 0, 0.0, r))
                lf.append(jnp.where(gz == 0, 0.0, f))
            made = []
            for s in range(2):
                t = 1 - s
                k = 2 * a + s
                h_new[0, k], h_new[1, k], h_new[2, k] = nr[s], nf[s], nz[s]
                gr = (signed[s] * nz[t]) * per_inner - RATIO * down_z(nf[s], lf[s])
                gf = RATIO * down_z(nr[s], lr[s]) - TIME_STEP * up_r(nz[s])
                gz_ = (up_r(inner * nf[s]) - signed[s] * nr[t]) * per_outer
                if base is None:
                    e_new[0, k], e_new[1, k], e_new[2, k] = er[s] + gr, ef[s] + gf, ez[s] + gz_
                else:
                    for c, g in enumerate((gr, gf, gz_)):
                        e_new[c, k] = base[c, k] + g
                made.append((gz_, gr, gf))
            if curl is not None:
                for s in range(2):
                    for c in range(3):
                        curl[c, 2 * a + s] = made[s][c]

                @pl.when(me * (OWN // 2) + a == 0)
                def _():
                    curl[0, 1] = made[0][2]
            return carry
        lax.fori_loop(0, OWN // 2, pair, 0)

    for copy in halo1:
        copy.wait_recv()
    maxwell(e0, h0, below1, above1, h1, x1, curl1)
    go2_start()

    for copy in loads[2:]:
        copy.wait()
    stiff, damp, couple, harden = (mat[i, 0] for i in range(4))
    over = 1.0 / (1.0 + 0.5 * damp)
    packed = jnp.concatenate(
        [(1.0 - 0.5 * damp) * over, stiff * couple * over, stiff * over, 0.1 * harden * over]
        + [jnp.zeros((124, R), F32)],
        axis=0,
    )
    for half in range(2):
        turned = packed[:, half * 128 : half * 128 + 128].T
        for i in range(4):
            coef[i, pl.ds(half * 128, 128), :] = jnp.broadcast_to(turned[:, i : i + 1], (128, 128))

    weight = jnp.where(
        lax.broadcasted_iota(jnp.int32, (M, 1), 0) == 0, 1.0 / NA, 2.0 / NA
    ).astype(F32)

    def unrotate(value, b):
        mode = lax.broadcasted_iota(jnp.int32, (OWN, 1), 0) + b * OWN
        per_order = jnp.where(mode < 2, 0.0, 1.0 / jnp.maximum((mode // 2).astype(F32), 1.0))
        turned = jnp.where(
            lax.rem(mode, 2) == 0, -pltpu.roll(value, OWN - 1, 0), pltpu.roll(value, 1, 0)
        )
        return mode, turned * per_order

    def block_rows(b):
        return pl.ds(pl.multiple_of(b * OWN, OWN), OWN)

    def gauge_psi():
        def block(b, carry):
            at = block_rows(b)
            psi[at, :] = jnp.where(y > 0, outer * ch1[1, at, :], 0.0)
            return carry
        lax.fori_loop(0, M // OWN, block, 0, unroll=4)

    def gauge_radial():
        def block(b, carry):
            at = block_rows(b)
            value = psi[at, :]
            gauge_r[at, :] = ch1[0, at, :] - unrotate(down_r(value), b)[1]
            return carry
        lax.fori_loop(0, M // OWN, block, 0, unroll=4)

    def gauge_axial():
        def block(b, carry):
            at = block_rows(b)
            step = jnp.where(y < 3, after[at, :], 0.0) - psi[at, :]
            mode, made = unrotate(step, b)
            value = ch1[2, at, :] - (RATIO / TIME_STEP) * made
            gauge_z[at, :] = jnp.where(mode == 1, pltpu.roll(ch1[1, at, :], 1, 0), value)
            return carry
        lax.fori_loop(0, M // OWN, block, 0, unroll=4)

    def complete():
        def block(b, carry):
            at = pl.ds(pl.multiple_of(b * OWN, OWN), OWN)
            axial, radial = f2[0, at, :], f2[1, at, :]
            total = up_r(inner * radial) + (RATIO / TIME_STEP) * (outer * (axial - before[at, :]))
            mode, made = unrotate(-total, b)
            f2[2, at, :] = jnp.where(mode == 0, pltpu.roll(axial, OWN - 1, 0), made)
            return carry
        lax.fori_loop(0, M // OWN, block, 0, unroll=4)

    def to_points(field, add, sub, first, last):
        def forward(c, carry):
            value = field[c] if sub is None else field[c] + (add[lax.rem(c + 1, 3)] - sub[c])
            pts[c] = dot3(split(value.T), (tab[0], tab[1]), ((1,), (0,)))
            return carry
        lax.fori_loop(first, last, forward, 0)

    def respond():
        def block(b, carry):
            at = pl.ds(pl.multiple_of(b * 8, 8), 8)
            keep, drive, pull, soft = (coef[i, at, :] for i in range(4))
            for q in range(NA // 128):
                n = pl.ds(q * 128, 128)
                p = [pol[c, at, n] for c in range(3)]
                v = [vel[c, at, n] for c in range(3)]
                u = [drive * pts[c, at, n] for c in range(3)]
                start = list(p)
                for _ in range(SUBSTEPS):
                    energy = p[0] * p[0] + p[1] * p[1] + p[2] * p[2]
                    rate = pull + soft * energy
                    for c in range(3):
                        v[c] = keep * v[c] + u[c] - rate * p[c]
                        p[c] = p[c] + v[c]
                for c in range(3):
                    pol[c, at, n] = p[c]
                    vel[c, at, n] = v[c]
                    pts[c, at, n] = p[c] - start[c]
            return carry
        lax.fori_loop(0, R // 8, block, 0, unroll=2)

    def to_modes(sub, change, first, last):
        def backward(c, carry):
            made = weight * dot3((tab[0], tab[1]), split(pts[c]), ((1,), (1,)))
            change[c] = made if sub is None else sub[c] + made
            return carry
        lax.fori_loop(first, last, backward, 0)

    go1[1]()
    to_points(f1, None, None, 0, 3)
    respond()
    to_modes(None, ch1, 1, 2)
    gauge_psi()
    pl.when(y > 0)(lambda: lead.start())
    pl.when(y == 0)(lambda: each_spread(lambda c: c.start()))
    to_modes(None, ch1, 0, 1)
    to_modes(None, ch1, 2, 3)
    gauge_radial()
    go2_wait_axial()
    pl.when(y < 3)(lambda: follow.start())
    go2_wait_rest()
    back_r[0]()
    pl.when(y < 3)(lambda: lead.wait_recv())
    gauge_axial()
    back_z[0]()
    pl.when(y > 0)(lambda: relayed(lambda c: c.wait_recv()))
    each_phi(lambda c, dz: c.start())
    to_points(f1, f2, ch1, 0, 1)
    to_points(f1, f2, ch1, 2, 3)

    @pl.when(y > 0)
    def _():
        follow.wait_recv()
        complete()

    to_points(f1, f2, ch1, 1, 2)
    respond()
    to_modes(ch1, ch2, 0, 3)
    back2[0]()
    back_r[1]()
    back_z[1]()
    each_phi(lambda c, dz: c.wait_recv() if dz else c.wait())

    def subtract(i, carry):
        for c in range(3):
            e1[c, i] = x1[c, i] - c1[(c + 1) % 3, i]
        return carry
    lax.fori_loop(0, OWN, subtract, 0)

    @pl.when(me == 0)
    def _():
        e1[1, 0] = x1[1, 0] - c1[0, 1]
        e1[2, 1] = x1[2, 1]

    for copy in halo2:
        copy.start()
    for copy in halo2:
        copy.wait_recv()
    maxwell(e1, h1, below2, above2, h2, x2, base=x1)

    back2[1]()

    def finish_e(i, carry):
        for c in range(3):
            x2[c, i] = x2[c, i] - c2[c, i]
        return carry
    lax.fori_loop(0, OWN, finish_e, 0)
    for stage in (go1, back_r, back_z, back2):
        stage[2]()
    go2_wait_send()
    pl.when(y < 3)(lambda: follow.wait_send())
    pl.when(y > 0)(lambda: lead.wait_send())
    pl.when(y == 0)(lambda: each_spread(lambda c: c.wait_send()))
    each_phi(lambda c, dz: c.wait_send() if dz else None)
    for copy in halo1 + halo2:
        copy.wait_send()


def finish(*refs):
    half, sem = len(refs) // 2, refs[-1]
    copies = [
        pltpu.make_async_copy(refs[i], refs[half + i], sem.at[i]) for i in range(half)
    ]
    for copy in copies:
        copy.start()
    for copy in copies:
        copy.wait()


def on_device(efield, hfield, polar, velocity, material):
    field = pltpu.VMEM((3, OWN, OWN, R), F32)
    state = pltpu.VMEM((3, R, NA), F32)
    modes = pltpu.VMEM((3, M, R), F32)
    dma = pltpu.SemaphoreType.DMA
    anywhere = pl.BlockSpec(memory_space=pl.ANY)
    results = [
        jax.ShapeDtypeStruct((3, OWN, OWN, R), F32),
        jax.ShapeDtypeStruct((3, OWN, OWN, R), F32),
        jax.ShapeDtypeStruct((3, R, NA), F32),
        jax.ShapeDtypeStruct((3, R, NA), F32),
    ]
    made = pl.pallas_call(
        kernel,
        out_shape=[pltpu.VMEM(r.shape, r.dtype) for r in results],
        in_specs=[anywhere] * 6,
        out_specs=[pl.BlockSpec(memory_space=pltpu.VMEM)] * 4,
        scratch_shapes=[field] * 8 + [modes] * 4
        + [state]
        + [
            pltpu.VMEM((4, 1, 1, R), F32),
            pltpu.VMEM((4, R, 128), F32),
            pltpu.VMEM((2, M, NA), BF16),
            pltpu.VMEM((5, OWN, R), F32),
            pltpu.VMEM((2, OWN, R), F32),
            pltpu.VMEM((5, OWN, R), F32),
            pltpu.VMEM((2, OWN, R), F32),
            pltpu.VMEM((M, R), F32),
            pltpu.VMEM((M, R), F32),
            pltpu.VMEM((M, R), F32),
            pltpu.VMEM((M, R), F32),
            pltpu.VMEM((M, R), F32),
            pltpu.VMEM((4, OWN, R), F32),
            dma((6,)), dma((7, OWN)), dma((7, OWN)), dma((7,)), dma((2, 3)), dma((2, 3)), dma((4,)),
            dma((OWN,)), dma((4,)),
        ],
        compiler_params=pltpu.CompilerParams(
            collective_id=0, has_side_effects=True, vmem_limit_bytes=59 << 20
        ),
        name="yee_gas",
    )(
        efield,
        hfield,
        polar.reshape(3, R, NA),
        velocity.reshape(3, R, NA),
        material,
        jnp.asarray(tables()),
    )
    new_e, new_h, new_p, new_v = pl.pallas_call(
        finish,
        out_shape=results,
        in_specs=[pl.BlockSpec(memory_space=pltpu.VMEM)] * 4,
        out_specs=[anywhere] * 4,
        scratch_shapes=[dma((4,))],
        compiler_params=pltpu.CompilerParams(vmem_limit_bytes=8 << 20),
        name="finish",
    )(*made)
    shape = (3, 1, 1, R, NA)
    return new_e, new_h, new_p.reshape(shape), new_v.reshape(shape)


def solution(mesh):
    field, state = P(None, "mode", "gz", None), P(None, "gz", "mode", None, None)
    return jax.shard_map(
        on_device,
        mesh=mesh,
        in_specs=(field, field, state, state, P(None, "gz", "mode", None)),
        out_specs=(field, field, state, state),
        check_vma=False,
    )
```
